32 devices in a mesh: ens: 2 (over y), tile: 4 (over z), trc: 2 (over x), lev: 2 (over core).
Axes of the slice: x: 2, y: 2, z: 4, core: 2. Of those that a mesh axis runs over, the one named last changes fastest.
Arguments:
- tracers: float32 [32, 16, 64, 128], P('trc', 'lev', ('ens', 'tile')), parts along dimension 2, may hold values from -6 to 6
- cotangent: float32 [32, 16, 64, 128], P('trc', 'lev', ('ens', 'tile')), parts along dimension 2, may hold values from -3 to 3
- zonal_speed: float32 [16, 64, 128], P('lev', ('ens', 'tile')), parts along dimension 1, may hold values from -0.3 to 0.3
- meridional_speed: float32 [16, 64, 128], P('lev', ('ens', 'tile')), parts along dimension 1, may hold values from -0.3 to 0.3
- vertical_speed: float32 [16, 64, 128], P('lev', ('ens', 'tile')), parts along dimension 1, may hold values from -0.3 to 0.3
- lateral_mixing: float32 [16, 64, 128], P('lev', ('ens', 'tile')), parts along dimension 1, may hold values from 0.01 to 0.08
- vertical_mixing: float32 [16, 64, 128], P('lev', ('ens', 'tile')), parts along dimension 1, may hold values from 0.02 to 0.16
- column_depth: int32 [64, 128], P(('ens', 'tile')), parts along dimension 0, may hold values from 0 to 16
Outputs:
- start_cotangent: float32 [32, 16, 64, 128], P('trc', 'lev', ('ens', 'tile')), parts along dimension 2
- speed_cotangent: float32 [3, 16, 64, 128], P(None, ('lev', 'trc'), ('ens', 'tile')), parts along dimension 2
The draws below stay inside these ranges and needn't reach their ends.
There are 2 independent parts, one for each index of `ens`. The reference program is written for one: setup_inputs(seed, part) draws one part's arguments, and reference() takes and returns one part's arrays. A program takes and returns all parts, laid end to end along the dimension named above; each array names one. Nothing has to cross between parts.
All inputs are finite; a program needn't handle non-finite values.
Results may differ from the reference program's by a relative error of at most 0.0003.
Values sent between devices are 32-bit elements; how exact they have to be, the bound alone decides.
No kernel may reach another device: no remote copies, remote signals or barrier semaphores. Data moves between devices by JAX's collectives and lax.ppermute only.
A program may use at most 64 MiB of HBM per device.

```python
import math
import jax
import jax.numpy as jnp
from jax import lax

LEVELS = 16
TRACERS = 32
NX = 32
NY = 128


def place_ends(values, own_key, smallest, largest):
    longest = values.shape.index(max(values.shape))
    spots = []
    for shift in (0, 1):
        where = [jax.random.randint(jax.random.fold_in(own_key, axis), (), 0, length) for axis, length in enumerate(values.shape)]
        where[longest] = (where[longest] + shift) % values.shape[longest]
        spots.append(tuple(where))
    return values.at[spots[0]].set(smallest).at[spots[1]].set(largest)


def block_scale(key, shape, shards, low, top_value):
    def one(position, blocks):
        draws = jax.random.uniform(jax.random.fold_in(jax.random.fold_in(key, 6), position), (blocks,), jnp.float32, low / len(shards), top_value / len(shards))
        return jnp.repeat(jnp.exp(draws), shape[position] // blocks).reshape((-1,) + (1,) * (len(shape) - position - 1))

    level = one(*shards[0])
    for cut in shards[1:]:
        level = level * one(*cut)
    return level


def noise(stream_key, dims, scale, most, split=(), held_as=jnp.bfloat16):
    gain = block_scale(stream_key, dims, split, -0.22, 0.18) if split else 1.0
    array = jax.random.normal(stream_key, dims, jnp.float32) * scale * gain
    return jnp.minimum(jnp.maximum(array, -most), most).astype(held_as)


def setup_inputs(seed: int = 0, part: int = 0) -> dict:
    streams_of = jax.random.split(jax.random.key(seed), 9)
    part_splits = jax.random.split(jax.random.fold_in(streams_of[8], part), 9)
    tracers = noise(part_splits[0], (TRACERS, LEVELS, NX, NY), 1.0, 6.0, ((0, 2), (1, 2), (2, 4)), jnp.float32)
    cotangent = noise(part_splits[1], (TRACERS, LEVELS, NX, NY), 0.5, 3.0, ((0, 2), (1, 2), (2, 4)), jnp.float32)
    zonal_speed = noise(part_splits[2], (LEVELS, NX, NY), 0.1, 0.3, ((0, 2), (1, 4)), jnp.float32)
    meridional_speed = noise(part_splits[3], (LEVELS, NX, NY), 0.1, 0.3, ((0, 2), (1, 4)), jnp.float32)
    vertical_speed = noise(part_splits[4], (LEVELS, NX, NY), 0.1, 0.3, ((0, 2), (1, 4)), jnp.float32)
    lateral_mixing = jnp.clip(jnp.exp(math.log(0.08) - 2.0794415 * jax.random.uniform(part_splits[5], (LEVELS, NX, NY), jnp.float32) ** block_scale(part_splits[5], (LEVELS, NX, NY), ((0, 2), (1, 4)), -0.2, 0.2)), 0.01, 0.08)
    vertical_mixing = jnp.clip(jnp.exp(math.log(0.16) - 2.0794415 * jax.random.uniform(part_splits[6], (LEVELS, NX, NY), jnp.float32) ** block_scale(part_splits[6], (LEVELS, NX, NY), ((0, 2), (1, 4)), -0.2, 0.2)), 0.02, 0.16)
    column_depth = place_ends(jax.random.randint(part_splits[7], (NX, NY), 0, LEVELS + 1), jax.random.fold_in(part_splits[7], 1), 0, LEVELS).astype(jnp.int32)
    return {"tracers": tracers, "cotangent": cotangent, "zonal_speed": zonal_speed, "meridional_speed": meridional_speed, "vertical_speed": vertical_speed, "lateral_mixing": lateral_mixing, "vertical_mixing": vertical_mixing, "column_depth": column_depth}


albada_floor = 0.01

def albada(lower_step, upper_step):
    return lower_step * upper_step * (lower_step + upper_step) / (lower_step * lower_step + upper_step * upper_step + albada_floor)

def face_flux(far_behind, behind, beyond, far_beyond, velocity, spread, opened):
    rising = behind + 0.5 * albada(behind - far_behind, beyond - behind)
    falling = beyond - 0.5 * albada(beyond - behind, far_beyond - beyond)
    carried = jnp.where(velocity >= 0.0, rising, falling)
    return opened * (velocity * carried - spread * (beyond - behind))

def window(values, direction, offset):
    leading = values.ndim - 3
    pieces = [slice(None)] * leading
    for spatial in range(3):
        extent = values.shape[leading + spatial] - 4
        if spatial == direction:
            pieces.append(slice(offset, extent + 1 + offset))
        else:
            pieces.append(slice(2, extent + 2))
    return values[tuple(pieces)]

def advance(padded, fields):
    wetness = fields[5]
    result = padded[:, 2:-2, 2:-2, 2:-2]
    for direction, speed_row, spread_row in ((0, 2, 4), (1, 0, 3), (2, 1, 3)):
        through = face_flux(window(padded, direction, 0), window(padded, direction, 1), window(padded, direction, 2), window(padded, direction, 3), window(fields[speed_row], direction, 2), window(fields[spread_row], direction, 2), window(wetness, direction, 1) * window(wetness, direction, 2))
        extent = through.shape[direction + 1]
        result = result + lax.slice_in_dim(through, 0, extent - 1, axis=direction + 1) - lax.slice_in_dim(through, 1, extent, axis=direction + 1)
    return result

def reference(tracers, cotangent, zonal_speed, meridional_speed, vertical_speed, lateral_mixing, vertical_mixing, column_depth):
    levels = tracers.shape[1]
    wetness = (jnp.arange(levels, dtype=jnp.int32)[:, None, None] < column_depth[None]).astype(jnp.float32)
    others = jnp.stack([lateral_mixing, vertical_mixing, wetness])
    speeds = jnp.stack([zonal_speed, meridional_speed, vertical_speed])

    def single(tracer_field, speed_set):
        padded = jnp.pad(tracer_field[None], ((0, 0), (2, 2), (2, 2), (2, 2)))
        fields = jnp.pad(jnp.concatenate([speed_set, others]), ((0, 0), (2, 2), (2, 2), (2, 2)))
        return advance(padded, fields)[0]

    def per_tracer(summed, slices):
        initial, final_cot = slices
        middle = single(initial, speeds)
        _, pull_late = jax.vjp(single, middle, speeds)
        middle_cot, late_speed = pull_late(final_cot)
        _, pull_early = jax.vjp(single, initial, speeds)
        start_cot, early_speed = pull_early(middle_cot)
        return (summed + late_speed + early_speed, start_cot)
    summed, start_cotangent = lax.scan(per_tracer, jnp.zeros_like(speeds), (tracers, cotangent))
    return (start_cotangent, summed)
```

```python
import functools

import jax
import jax.numpy as jnp
from jax import lax
from jax.experimental import pallas as pl
from jax.experimental.pallas import tpu as pltpu
from jax.sharding import PartitionSpec as P

albada_floor = 0.01
H = 4
E = 2
W = 3
NF = 5
FPAD = 16


def pairings(count):
    phases = []
    for first in (0, 1):
        pairs = []
        for i in range(first, count - 1, 2):
            pairs += [(i, i + 1), (i + 1, i)]
        if pairs:
            phases.append(pairs)
    return phases


def by_parity(even, phase, act):
    @pl.when(even)
    def _():
        act(phase == 0)

    @pl.when(jnp.logical_not(even))
    def _():
        act(phase == 1)


def pack_body(dims, n_tile, n_lev, idx_ref, q_ref, l_ref, *refs):
    T, L, C, Y = dims
    f_refs, depth_ref = refs[:NF], refs[NF]
    tile_out = refs[NF + 1 : NF + 1 + n_tile]
    lev_out = refs[NF + 1 + n_tile :]
    tile_even = idx_ref[0] == 0
    lev_even = idx_ref[1] == 0

    def slab(ref, k, c):
        return ref[pl.ds(k * C + c, T, stride=L * C), :]

    for phase, out in enumerate(tile_out):

        def send_tile(high, out=out):
            q0 = C - H if high else 0
            l0 = C - E if high else 0
            f0 = C - W if high else 0

            def level(k, carry):
                for j in range(H):
                    out[k, j * T : (j + 1) * T, :] = slab(q_ref, k, q0 + j)
                for j in range(E):
                    out[k, (H + j) * T : (H + j + 1) * T, :] = slab(l_ref, k, l0 + j)
                base = (H + E) * T
                for f in range(NF):
                    out[k, base + W * f : base + W * (f + 1), :] = f_refs[f][k, f0 : f0 + W, :]
                out[k, base + W * NF : base + W * NF + 1, :] = depth_ref[f0 : f0 + 1, :].astype(jnp.float32)
                return carry

            lax.fori_loop(0, L, level, 0)
            base = (H + E) * T + W * NF
            for j in range(1, W):
                out[j, base : base + 1, :] = depth_ref[f0 + j : f0 + j + 1, :].astype(jnp.float32)

        by_parity(tile_even, phase, send_tile)

    for phase, out in enumerate(lev_out):

        def send_lev(high, out=out):
            def column(c, carry):
                for j in range(H):
                    k = (L - H if high else 0) + j
                    out[j, pl.ds(pl.multiple_of(c * T, 8), T), :] = slab(q_ref, k, c)
                for j in range(E):
                    k = (L - E if high else 0) + j
                    out[H + j, pl.ds(pl.multiple_of(c * T, 8), T), :] = slab(l_ref, k, c)
                return carry

            lax.fori_loop(0, C, column, 0)
            for j in range(W):
                k = (L - W if high else 0) + j
                for f in range(NF):
                    out[H + E, (j * NF + f) * C : (j * NF + f + 1) * C, :] = f_refs[f][k]

        by_parity(lev_even, phase, send_lev)


def limiter(x, y, xx, yy):
    s = x * y
    r = 1.0 / (xx + yy + albada_floor)
    a = s * (x + y) * r
    return s, r, a


def forward_chain(n, get_u, get_co, emit):
    u_a, u_b = get_u(-2), get_u(-1)
    d_b = u_b - u_a
    xx_b = d_b * d_b
    half_b = None
    flux_b = None
    for f in range(0, n + 2):
        u_c = get_u(f)
        d_c = u_c - u_b
        xx_c = d_c * d_c
        _, _, a = limiter(d_b, d_c, xx_b, xx_c)
        half_c = 0.5 * a
        if f >= 1:
            v, m = get_co(f - 1)
            carried = jnp.where(v >= 0.0, u_a + half_b, u_b - half_c)
            flux = v * carried - m * d_b
            if f >= 2:
                emit(f - 2, flux_b - flux)
            flux_b = flux
        u_a, u_b, d_b, xx_b, half_b = u_b, u_c, d_c, xx_c, half_c


def adjoint_chain(n, get_u, get_l, get_co, emit, emit_speed):
    u_a, u_b = get_u(-2), get_u(-1)
    l_a, l_b = get_l(-2), get_l(-1)
    d_b = u_b - u_a
    xx_b = d_b * d_b
    hh_b = 0.5 * xx_b
    g_b = l_b - l_a
    v, m = get_co(-1)
    v_b = v
    n_b = jnp.minimum(v, 0.0) * g_b
    p_b = dm_b = None
    half_b = None
    down_a = None
    dd_a = None
    n_a = None
    for f in range(0, n + 2):
        u_c, l_c = get_u(f), get_l(f)
        d_c = u_c - u_b
        xx_c = d_c * d_c
        hh_c = 0.5 * xx_c
        g_c = l_c - l_b
        v_c, m_c = get_co(f)
        p_c = jnp.maximum(v_c, 0.0) * g_c
        n_c = jnp.minimum(v_c, 0.0) * g_c
        s, r, a = limiter(d_b, d_c, xx_b, xx_c)
        half_c = 0.5 * a
        er = (p_c - n_b) * r
        if f >= 1:
            x_c = er * (hh_c + s - d_b * a)
            dd_b = x_c + down_a - dm_b
            if f >= 2:
                emit(f - 2, n_a + p_b + dd_a - dd_b)
            if f - 1 < n:
                carried = jnp.where(v_b >= 0.0, u_a + half_b, u_b - half_c)
                emit_speed(f - 1, g_b * carried)
            dd_a = dd_b
        down_a = er * (hh_b + s - d_c * a)
        n_a = n_b
        p_b, n_b, v_b = p_c, n_c, v_c
        dm_b = m_c * g_c
        g_b = g_c
        half_b = half_c
        u_a, u_b, l_b, d_b, xx_b, hh_b = u_b, u_c, l_c, d_c, xx_c, hh_c


def lanes(T, Y):
    lane = lax.broadcasted_iota(jnp.int32, (T, Y), 1)
    return lane == 0, lane == Y - 1


def along_forward(u, v, m, first, last, Y):
    before = jnp.where(first, 0.0, pltpu.roll(u, 1, 1))
    d = u - before
    nxt = jnp.where(last, -u, pltpu.roll(d, Y - 1, 1))
    _, _, a = limiter(d, nxt, d * d, nxt * nxt)
    half = 0.5 * a
    carried = jnp.where(v >= 0.0, before + pltpu.roll(half, 1, 1), u - half)
    flux = v * carried - m * d
    return flux - pltpu.roll(flux, Y - 1, 1)


def along_adjoint(u, l, v, m, first, last, Y):
    before = jnp.where(first, 0.0, pltpu.roll(u, 1, 1))
    d = u - before
    nxt = jnp.where(last, -u, pltpu.roll(d, Y - 1, 1))
    xx, yy = d * d, nxt * nxt
    s, r, a = limiter(d, nxt, xx, yy)
    half = 0.5 * a
    g = l - pltpu.roll(l, 1, 1)
    p = jnp.maximum(v, 0.0) * g
    n = jnp.minimum(v, 0.0) * g
    er = (pltpu.roll(p, Y - 1, 1) - n) * r
    z = er * (0.5 * yy + s - d * a) - m * g
    down = er * (0.5 * xx + s - nxt * a)
    carried = jnp.where(v >= 0.0, before + pltpu.roll(half, 1, 1), u - half)
    add = (
        (n + z - down)
        + jnp.where(first, 0.0, pltpu.roll(down, 1, 1))
        + jnp.where(last, 0.0, pltpu.roll(p - z, Y - 1, 1))
    )
    return add, g * carried


class Fields:
    def __init__(self, f_ref, d_ref, level0):
        self.f, self.d, self.level0 = f_ref, d_ref, level0

    def at(self, direction, k, c):
        depth = self.d[direction, W + c]
        level = (self.level0 + k).astype(jnp.float32)
        if direction == 2:
            level = jnp.where(level >= 1.0, level, 1e9)
        is_open = depth > level
        speed = self.f[(0, 1, 2)[direction], W + k, W + c]
        mix = self.f[(3, 3, 4)[direction], W + k, W + c]
        return jnp.where(is_open, speed, 0.0), jnp.where(is_open, mix, 0.0), is_open


def adjoint(dims, fields, u_ref, u_off, l_ref, acc_ref, done, speed_ref):
    T, L, C, Y = dims
    first, last = lanes(T, Y)
    uo = u_off

    def store_speed(direction, k, c, is_open, value):
        row = jnp.sum(value, axis=0, keepdims=True)
        speed_ref[direction, k, pl.ds(c, 1), :] = jnp.where(is_open, row, 0.0)

    def level(k, carry):
        for c in range(C):
            l = l_ref[E + k, E + c]
            v, m, is_open = fields.at(1, k, c)
            add, sp = along_adjoint(u_ref[uo + k, uo + c], l, v, m, first, last, Y)
            acc_ref[k, c] = l + add
            store_speed(1, k, c, is_open, sp)
        return carry

    lax.fori_loop(0, L, level, 0)

    def level_z(k, carry):
        opened = {}

        def co(c):
            v, m, opened[c] = fields.at(0, k, c)
            return v, m

        def emit(c, value):
            acc_ref[k, c] = acc_ref[k, c] + value

        adjoint_chain(
            C,
            lambda c: u_ref[uo + k, uo + c],
            lambda c: l_ref[E + k, E + c],
            co,
            emit,
            lambda c, value: store_speed(0, k, c, opened[c], value),
        )
        return carry

    lax.fori_loop(0, L, level_z, 0)

    def column_v(c, carry):
        opened = {}

        def co(k):
            v, m, opened[k] = fields.at(2, k, c)
            return v, m

        def emit(k, value):
            done(k, c, acc_ref[k, c] + value)

        adjoint_chain(
            L,
            lambda k: u_ref[uo + k, uo + c],
            lambda k: l_ref[E + k, E + c],
            co,
            emit,
            lambda k, value: store_speed(2, k, c, opened[k], value),
        )
        return carry

    lax.fori_loop(0, C, column_v, 0)


def middle_body(dims, n_tile, n_lev, idx_ref, q_ref, l_ref, *refs):
    T, L, C, Y = dims
    f_refs, depth_ref = refs[:NF], refs[NF]
    at = NF + 1
    tile_in = refs[at : at + n_tile]
    lev_in = refs[at + n_tile : at + n_tile + n_lev]
    corner_in = refs[at + n_tile + n_lev : at + n_tile + 2 * n_lev]
    at += n_tile + 2 * n_lev
    qe, fe, de, mc_ref, sp_ref = refs[at : at + 5]
    at += 5
    tile_out = refs[at : at + n_tile]
    lev_out = refs[at + n_tile : at + n_tile + n_lev]
    le, me = refs[at + n_tile + n_lev :]
    tile_even = idx_ref[0] == 0
    lev_even = idx_ref[1] == 0
    level0 = idx_ref[2]

    def own_level(k, carry):
        for c in range(C):
            qe[H + k, H + c] = q_ref[pl.ds(k * C + c, T, stride=L * C), :]
            le[E + k, E + c] = l_ref[pl.ds(k * C + c, T, stride=L * C), :]
            for f in range(NF):
                fe[f, W + k, W + c] = f_refs[f][k, c : c + 1, :]
        return carry

    lax.fori_loop(0, L, own_level, 0)
    depths = {}
    for c in range(C):
        depths[c] = depth_ref[c : c + 1, :].astype(jnp.float32)
        de[2, W + c] = depths[c]

    zero = jnp.zeros((T, Y), jnp.float32)
    zero_row = jnp.zeros((1, Y), jnp.float32)

    def place_tile(source, high):
        q0 = H + C if high else 0
        l0 = E + C if high else 0
        f0 = W + C if high else 0

        def level(k, carry):
            for j in range(H):
                qe[H + k, q0 + j] = zero if source is None else source[k, j * T : (j + 1) * T, :]
            for j in range(E):
                le[E + k, l0 + j] = zero if source is None else source[k, (H + j) * T : (H + j + 1) * T, :]
            base = (H + E) * T
            for f in range(NF):
                for j in range(W):
                    r = base + W * f + j
                    fe[f, W + k, f0 + j] = zero_row if source is None else source[k, r : r + 1, :]
            return carry

        lax.fori_loop(0, L, level, 0)
        base = (H + E) * T + W * NF
        for j in range(W):
            de[2, f0 + j] = zero_row if source is None else source[j, base : base + 1, :]

    def place_lev(source, high):
        q0 = H + L if high else 0
        l0 = E + L if high else 0
        f0 = W + L if high else 0

        def column(c, carry):
            rows = pl.ds(pl.multiple_of(c * T, 8), T)
            for j in range(H):
                qe[q0 + j, H + c] = zero if source is None else source[j, rows, :]
            for j in range(E):
                le[l0 + j, E + c] = zero if source is None else source[H + j, rows, :]
            return carry

        lax.fori_loop(0, C, column, 0)
        for j in range(W):
            for f in range(NF):
                for c in range(C):
                    r = (j * NF + f) * C + c
                    fe[f, f0 + j, W + c] = zero_row if source is None else source[H + E, r : r + 1, :]

    def place_corner(source, tile_high, lev_high):
        for j in range(E):
            q_lev = H + L + j if lev_high else H - E + j
            f_lev = W + L + j if lev_high else W - E + j
            for i in range(E):
                if source is None:
                    qe[q_lev, (H + C + i) if tile_high else (H - E + i)] = zero
                else:
                    s = i if tile_high else H - E + i
                    qe[q_lev, (H + C + i) if tile_high else (H - E + i)] = source[j, s * T : (s + 1) * T, :]
                for f in range(NF):
                    col = (W + C + i) if tile_high else (W - E + i)
                    if source is None:
                        fe[f, f_lev, col] = zero_row
                    else:
                        r = (H + E) * T + W * f + (i if tile_high else W - E + i)
                        fe[f, f_lev, col] = source[j, r : r + 1, :]

    def zero_corners(lev_high):
        for tile_high in (False, True):
            place_corner(None, tile_high, lev_high)

    for phase in range(2):
        by_parity(
            tile_even, phase, lambda high, p=phase: place_tile(tile_in[p] if p < n_tile else None, high)
        )
        by_parity(lev_even, phase, lambda high, p=phase: place_lev(lev_in[p] if p < n_lev else None, high))
        if phase >= n_lev:
            by_parity(lev_even, phase, zero_corners)
        else:
            for other in range(2):

                def corner(lev_high, p=phase, t=other):
                    source = corner_in[p].at[t] if t < n_tile else None
                    by_parity(tile_even, t, lambda tile_high: place_corner(source, tile_high, lev_high))

                by_parity(lev_even, phase, corner)

    lane0 = lax.broadcasted_iota(jnp.int32, (1, Y), 1) == 0
    de[0, 0] = zero_row
    de[1, 0] = zero_row
    for c in range(1, C + 2 * W):
        here = de[2, c]
        de[0, c] = jnp.minimum(de[2, c - 1], here)
        de[1, c] = jnp.where(lane0, 0.0, jnp.minimum(pltpu.roll(here, 1, 1), here))

    fields = Fields(fe, de, level0)
    first, last = lanes(T, Y)

    def along(k, c):
        u = qe[H + k, H + c]
        v, m, _ = fields.at(1, k, c)
        me[E + k, E + c] = u + along_forward(u, v, m, first, last, Y)

    def own_y(k, carry):
        for c in range(-E, C + E):
            along(k, c)
        return carry

    lax.fori_loop(0, L, own_y, 0)

    def zonal(k, c0, n):
        def emit(c, value):
            me[E + k, E + c0 + c] = me[E + k, E + c0 + c] + value

        forward_chain(
            n, lambda c: qe[H + k, H + c0 + c], lambda c: fields.at(0, k, c0 + c)[:2], emit
        )

    def own_z(k, carry):
        zonal(k, -E, C + 2 * E)
        return carry

    lax.fori_loop(0, L, own_z, 0)

    for phase in range(2):
        if phase < n_lev:
            high = lev_even if phase == 0 else jnp.logical_not(lev_even)
            k0 = jnp.where(high, L, -E)

            def beside(j, carry, k0=k0):
                for c in range(C):
                    along(k0 + j, c)
                zonal(k0 + j, 0, C)
                return carry

            lax.fori_loop(0, E, beside, 0)
        else:

            def blank(high):
                def column(c, carry):
                    for j in range(E):
                        me[(E + L if high else 0) + j, E + c] = zero
                    return carry

                lax.fori_loop(0, C, column, 0)

            by_parity(lev_even, phase, blank)

    def vertical(c, k0, n):
        def emit(k, value):
            me[E + k0 + k, E + c] = me[E + k0 + k, E + c] + value

        forward_chain(
            n, lambda k: qe[H + k0 + k, H + c], lambda k: fields.at(2, k0 + k, c)[:2], emit
        )

    def own_v(c, carry):
        vertical(c, -E, L + 2 * E)
        return carry

    lax.fori_loop(0, C, own_v, 0)

    def side_v(i, carry):
        vertical(jnp.where(i < E, i - E, C - E + i), 0, L)
        return carry

    lax.fori_loop(0, 2 * E, side_v, 0)

    def done(k, c, value):
        mc_ref[k, c] = value

    adjoint(dims, fields, me, E, le, mc_ref, done, sp_ref)

    for phase, out in enumerate(tile_out):

        def send_tile(high, out=out):
            def level(k, carry):
                for j in range(E):
                    out[k, j] = mc_ref[k, (C - E if high else 0) + j]
                return carry

            lax.fori_loop(0, L, level, 0)

        by_parity(tile_even, phase, send_tile)
    for phase, out in enumerate(lev_out):

        def send_lev(high, out=out):
            def column(c, carry):
                for j in range(E):
                    out[j, c] = mc_ref[(L - E if high else 0) + j, c]
                return carry

            lax.fori_loop(0, C, column, 0)

        by_parity(lev_even, phase, send_lev)


def start_body(dims, n_tile, n_lev, idx_ref, qe, fe, de, mc_ref, late_ref, *refs):
    T, L, C, Y = dims
    tile_in = refs[:n_tile]
    lev_in = refs[n_tile : n_tile + n_lev]
    out_ref, sp_ref, le, acc = refs[n_tile + n_lev :]
    tile_even = idx_ref[0] == 0
    lev_even = idx_ref[1] == 0
    zero = jnp.zeros((T, Y), jnp.float32)

    def own(k, carry):
        for c in range(C):
            le[E + k, E + c] = mc_ref[k, c]
        return carry

    lax.fori_loop(0, L, own, 0)

    def place_tile(source, high):
        def level(k, carry):
            for j in range(E):
                le[E + k, (E + C if high else 0) + j] = zero if source is None else source[k, j]
            return carry

        lax.fori_loop(0, L, level, 0)

    def place_lev(source, high):
        def column(c, carry):
            for j in range(E):
                le[(E + L if high else 0) + j, E + c] = zero if source is None else source[j, c]
            return carry

        lax.fori_loop(0, C, column, 0)

    for phase in range(2):
        by_parity(
            tile_even, phase, lambda high, p=phase: place_tile(tile_in[p] if p < n_tile else None, high)
        )
        by_parity(lev_even, phase, lambda high, p=phase: place_lev(lev_in[p] if p < n_lev else None, high))

    def done(k, c, value):
        out_ref[pl.ds(k * C + c, T, stride=L * C), :] = value

    adjoint(dims, Fields(fe, de, idx_ref[2]), qe, H, le, acc, done, sp_ref)
    sp_ref[...] = sp_ref[...] + late_ref[...]


def f32(*shape):
    return jax.ShapeDtypeStruct(shape, jnp.float32)


def call(body, name, n_in, outs, scratch, *args):
    vmem = pl.BlockSpec(memory_space=pltpu.VMEM)
    return pl.pallas_call(
        body,
        name=name,
        out_shape=outs,
        in_specs=[pl.BlockSpec(memory_space=pltpu.SMEM)] + [vmem] * (n_in - 1),
        out_specs=[vmem] * len(outs),
        scratch_shapes=scratch,
        compiler_params=pltpu.CompilerParams(vmem_limit_bytes=48 * 1024 * 1024),
    )(*args)


def share_speeds(values):
    count = lax.axis_size("trc")
    if count != 2:
        return lax.psum_scatter(values, "trc", scatter_dimension=1, tiled=True)
    half = values.shape[1] // 2
    me = lax.axis_index("trc")
    kept = lax.dynamic_slice_in_dim(values, me * half, half, axis=1)
    given = lax.dynamic_slice_in_dim(values, (1 - me) * half, half, axis=1)
    return kept + lax.ppermute(given, "trc", [(0, 1), (1, 0)])


def body(tracers, cotangent, zonal_speed, meridional_speed, vertical_speed, lateral_mixing, vertical_mixing, column_depth):
    dims = T, L, C, Y = tracers.shape
    tile_pairs = pairings(lax.axis_size("tile"))
    lev_pairs = pairings(lax.axis_size("lev"))
    n_tile, n_lev = len(tile_pairs), len(lev_pairs)
    tile, lev = lax.axis_index("tile"), lax.axis_index("lev")
    idx = jnp.stack([tile % 2, lev % 2, lev * L]).astype(jnp.int32)
    q = tracers.reshape(T * L * C, Y)
    l = cotangent.reshape(T * L * C, Y)
    inputs = (q, l, zonal_speed, meridional_speed, vertical_speed, lateral_mixing, vertical_mixing, column_depth)

    tile_rows = (H + E) * T + FPAD
    lev_rows = max(C * T, W * NF * C)
    outs = [f32(L, tile_rows, Y)] * n_tile + [f32(H + E + 1, lev_rows, Y)] * n_lev
    packed = call(functools.partial(pack_body, dims, n_tile, n_lev), "pack", 9, outs, [], idx, *inputs)
    from_tile = [lax.ppermute(x, "tile", p) for x, p in zip(packed[:n_tile], tile_pairs)]
    from_lev = [lax.ppermute(x, "lev", p) for x, p in zip(packed[n_tile:], lev_pairs)]
    corners = []
    for phase, pairs in enumerate(lev_pairs):
        k0 = jnp.where((lev + phase) % 2 == 0, L - E, 0)
        edge = jnp.stack([lax.dynamic_slice_in_dim(x, k0, E, axis=0) for x in from_tile])
        corners.append(lax.ppermute(edge, "lev", pairs))

    ext = (L + 2 * E, C + 2 * E, T, Y)
    outs = [
        f32(L + 2 * H, C + 2 * H, T, Y),
        f32(NF, L + 2 * W, C + 2 * W, 1, Y),
        f32(3, C + 2 * W, 1, Y),
        f32(L, C, T, Y),
        f32(3, L, C, Y),
    ]
    outs += [f32(L, E, T, Y)] * n_tile + [f32(E, C, T, Y)] * n_lev
    qe, fe, de, mc, late, *edges = call(
        functools.partial(middle_body, dims, n_tile, n_lev),
        "middle",
        9 + n_tile + 2 * n_lev,
        outs,
        [pltpu.VMEM(ext, jnp.float32)] * 2,
        idx,
        *inputs,
        *from_tile,
        *from_lev,
        *corners,
    )
    mc_tile = [lax.ppermute(x, "tile", p) for x, p in zip(edges[:n_tile], tile_pairs)]
    mc_lev = [lax.ppermute(x, "lev", p) for x, p in zip(edges[n_tile:], lev_pairs)]
    start, speeds = call(
        functools.partial(start_body, dims, n_tile, n_lev),
        "start",
        6 + n_tile + n_lev,
        [f32(T * L * C, Y), f32(3, L, C, Y)],
        [pltpu.VMEM(ext, jnp.float32), pltpu.VMEM((L, C, T, Y), jnp.float32)],
        idx,
        qe,
        fe,
        de,
        mc,
        late,
        *mc_tile,
        *mc_lev,
    )
    return start.reshape(T, L, C, Y), share_speeds(speeds)


def solution(mesh):
    return jax.shard_map(
        body,
        mesh=mesh,
        in_specs=(
            P("trc", "lev", ("ens", "tile"), None),
            P("trc", "lev", ("ens", "tile"), None),
            P("lev", ("ens", "tile"), None),
            P("lev", ("ens", "tile"), None),
            P("lev", ("ens", "tile"), None),
            P("lev", ("ens", "tile"), None),
            P("lev", ("ens", "tile"), None),
            P(("ens", "tile"), None),
        ),
        out_specs=(
            P("trc", "lev", ("ens", "tile"), None),
            P(None, ("lev", "trc"), ("ens", "tile"), None),
        ),
        check_vma=False,
    )
```

```python
import functools

import jax
import jax.numpy as jnp
from jax import lax
from jax.experimental import pallas as pl
from jax.experimental.pallas import tpu as pltpu
from jax.sharding import PartitionSpec as P

albada_floor = 0.01
H = 4
E = 2
W = 3
NF = 5
YC = 8
MIB = 60
FPAD = 16


def pairings(count):
    phases = []
    for first in (0, 1):
        pairs = []
        for i in range(first, count - 1, 2):
            pairs += [(i, i + 1), (i + 1, i)]
        if pairs:
            phases.append(pairs)
    return phases


def by_parity(even, phase, act):
    @pl.when(even)
    def _():
        act(phase == 0)

    @pl.when(jnp.logical_not(even))
    def _():
        act(phase == 1)


def limiter(x, y, xx, yy):
    s = x * y
    r = 1.0 / (xx + yy + albada_floor)
    a = s * (x + y) * r
    return s, r, a


def slopes(x, y, xx, yy, s, r, a):
    return r * (0.5 * yy + s - x * a), r * (0.5 * xx + s - y * a)


def forward_chain(n, get_u, get_co, emit, keep=None):
    u_a, u_b = get_u(-2), get_u(-1)
    d_b = u_b - u_a
    xx_b = d_b * d_b
    half_b = None
    flux_b = None
    for f in range(0, n + 2):
        u_c = get_u(f)
        d_c = u_c - u_b
        xx_c = d_c * d_c
        s, r, a = limiter(d_b, d_c, xx_b, xx_c)
        half_c = 0.5 * a
        carried = None
        if f >= 1:
            v, m = get_co(f - 1)
            carried = jnp.where(v >= 0.0, u_a + half_b, u_b - half_c)
            flux = v * carried - m * d_b
            if f >= 2:
                emit(f - 2, flux_b - flux)
            flux_b = flux
        if keep is not None:
            keep(f - 1, lambda: slopes(d_b, d_c, xx_b, xx_c, s, r, a), carried)
        u_a, u_b, d_b, xx_b, half_b = u_b, u_c, d_c, xx_c, half_c


def fresh_limits(get_u):
    state = {"u_a": get_u(-2), "u_b": get_u(-1), "half": None}
    state["d"] = state["u_b"] - state["u_a"]
    state["xx"] = state["d"] * state["d"]

    def step(f, v):
        u_a, u_b, d_b, xx_b = state["u_a"], state["u_b"], state["d"], state["xx"]
        u_c = get_u(f)
        d_c = u_c - u_b
        xx_c = d_c * d_c
        s, r, a = limiter(d_b, d_c, xx_b, xx_c)
        half_c = 0.5 * a
        carried = None
        if f >= 1:
            carried = jnp.where(v >= 0.0, u_a + state["half"], u_b - half_c)
        state.update(u_a=u_b, u_b=u_c, half=half_c, d=d_c, xx=xx_c)
        up, down = slopes(d_b, d_c, xx_b, xx_c, s, r, a)
        return up, down, carried

    return step


def adjoint_chain(n, limits, get_l, get_co, emit, emit_speed):
    l_b = get_l(-1)
    g_b = l_b - get_l(-2)
    v_b, _ = get_co(-1)
    n_b = jnp.minimum(v_b, 0.0) * g_b
    p_b = dm_b = down_a = dd_a = n_a = None
    for f in range(0, n + 2):
        l_c = get_l(f)
        g_c = l_c - l_b
        v_c, m_c = get_co(f)
        p_c = jnp.maximum(v_c, 0.0) * g_c
        n_c = jnp.minimum(v_c, 0.0) * g_c
        up, down, carried = limits(f, v_b)
        e = p_c - n_b
        if f >= 1:
            dd_b = e * up + down_a - dm_b
            if f >= 2:
                emit(f - 2, n_a + p_b + dd_a - dd_b)
            if f - 1 < n:
                emit_speed(f - 1, g_b * carried)
            dd_a = dd_b
        down_a = e * down
        n_a = n_b
        p_b, n_b, v_b = p_c, n_c, v_c
        dm_b = m_c * g_c
        g_b, l_b = g_c, l_c


def lanes(T, Y):
    lane = lax.broadcasted_iota(jnp.int32, (T, Y), 1)
    return lane == 0, lane == Y - 1


def along_values(u, v, ends):
    first, last = ends
    Y = u.shape[-1]
    before = jnp.where(first, 0.0, pltpu.roll(u, 1, 1))
    d = u - before
    nxt = jnp.where(last, -u, pltpu.roll(d, Y - 1, 1))
    xx, yy = d * d, nxt * nxt
    s, r, a = limiter(d, nxt, xx, yy)
    half = 0.5 * a
    carried = jnp.where(v >= 0.0, before + pltpu.roll(half, 1, 1), u - half)
    return d, carried, lambda: slopes(d, nxt, xx, yy, s, r, a)


def along_forward(d, carried, v, m):
    flux = v * carried - m * d
    return flux - pltpu.roll(flux, flux.shape[-1] - 1, 1)


def along_adjoint(l, v, m, up, down, ends):
    first, last = ends
    Y = l.shape[-1]
    g = l - pltpu.roll(l, 1, 1)
    p = jnp.maximum(v, 0.0) * g
    n = jnp.minimum(v, 0.0) * g
    e = pltpu.roll(p, Y - 1, 1) - n
    z = e * up - m * g
    y = e * down
    add = (
        (n + z - y)
        + jnp.where(first, 0.0, pltpu.roll(y, 1, 1))
        + jnp.where(last, 0.0, pltpu.roll(p - z, Y - 1, 1))
    )
    return add, g


class Fields:
    def __init__(self, f_ref, d_ref, level0):
        self.f, self.d, self.level0 = f_ref, d_ref, level0

    def at(self, direction, k, c):
        depth = self.d[direction, W + c]
        level = (self.level0 + k).astype(jnp.float32)
        if direction == 2:
            level = jnp.where(level >= 1.0, level, 1e9)
        is_open = depth > level
        speed = self.f[direction, W + k, W + c]
        mix = self.f[(3, 3, 4)[direction], W + k, W + c]
        return jnp.where(is_open, speed, 0.0), jnp.where(is_open, mix, 0.0), is_open


def parities():
    return lax.axis_index("tile") % 2 == 0, lax.axis_index("lev") % 2 == 0


def depth_rows(de, columns):
    Y = de.shape[-1]
    lane0 = lax.broadcasted_iota(jnp.int32, (1, Y), 1) == 0
    for c in columns:
        here = de[2, W + c]
        de[1, W + c] = jnp.where(lane0, 0.0, jnp.minimum(pltpu.roll(here, 1, 1), here))


def fetch(pairs, sem):
    copies = [pltpu.make_async_copy(a, b, sem.at[i]) for i, (a, b) in enumerate(pairs)]
    for c in copies:
        c.start()
    return copies


def edges_body(dims, n_tile, *refs):
    T, L, C, _ = dims
    sources, tile_out, (q_ref, l_ref, f_ref, d_ref, sem) = refs[:8], refs[8 : 8 + n_tile], refs[8 + n_tile :]
    targets = [q_ref, l_ref] + [f_ref.at[f] for f in range(NF)] + [d_ref]
    copies = fetch(zip(sources, targets), sem)
    for c in copies[2:] + copies[:2]:
        c.wait()
    tile_even, _ = parities()

    def slab(ref, k, c):
        return ref[pl.ds(k * C + c, T, stride=L * C), :]

    for phase, out in enumerate(tile_out):

        def send_tile(high, out=out):
            q0 = C - H if high else 0
            l0 = C - E if high else 0
            f0 = C - W if high else 0

            def level(k, carry):
                for j in range(H):
                    out[k, j * T : (j + 1) * T, :] = slab(q_ref, k, q0 + j)
                for j in range(E):
                    out[k, (H + j) * T : (H + j + 1) * T, :] = slab(l_ref, k, l0 + j)
                base = (H + E) * T
                for f in range(NF):
                    out[k, base + W * f : base + W * (f + 1), :] = f_ref[f, k, f0 : f0 + W, :]
                out[k, base + W * NF : base + W * NF + 1, :] = d_ref[f0 : f0 + 1, :].astype(jnp.float32)
                return carry

            lax.fori_loop(0, L, level, 0, unroll=2)
            base = (H + E) * T + W * NF
            for j in range(1, W):
                out[j, base : base + 1, :] = d_ref[f0 + j : f0 + j + 1, :].astype(jnp.float32)

        by_parity(tile_even, phase, send_tile)


def own_body(dims, n_lev, *refs):
    T, L, C, Y = dims
    sources, lev_out = refs[:8], refs[9 : 9 + n_lev]
    qe, le, fe, de, q_ref, l_ref, f_ref, d_ref, sem = refs[9 + n_lev :]
    targets = [q_ref, l_ref] + [f_ref.at[f] for f in range(NF)] + [d_ref]
    copies = fetch(zip(sources, targets), sem)
    for c in copies[2:] + copies[:2]:
        c.wait()
    _, lev_even = parities()
    zero = jnp.zeros((T, Y), jnp.float32)
    zero_row = jnp.zeros((1, Y), jnp.float32)

    def own_level(k, carry):
        for c in range(C):
            qe[H + k, H + c] = q_ref[pl.ds(k * C + c, T, stride=L * C), :]
            le[E + k, E + c] = l_ref[pl.ds(k * C + c, T, stride=L * C), :]
            for f in range(NF):
                fe[f, W + k, W + c] = f_ref[f, k, c : c + 1, :]
        return carry

    lax.fori_loop(0, L, own_level, 0)
    for c in range(C):
        de[2, W + c] = d_ref[c : c + 1, :].astype(jnp.float32)
    depth_rows(de, range(C))

    for phase, out in enumerate(lev_out):

        def send_lev(high, out=out):
            def column(c, carry):
                rows = pl.ds(pl.multiple_of(c * T, 8), T)
                for j in range(H):
                    out[j, rows, :] = qe[H + (L - H if high else 0) + j, H + c]
                for j in range(E):
                    out[H + j, rows, :] = le[E + (L - E if high else 0) + j, E + c]
                return carry

            lax.fori_loop(0, C, column, 0)
            for j in range(W):
                k = (L - W if high else 0) + j
                for f in range(NF):
                    out[H + E, (j * NF + f) * C : (j * NF + f + 1) * C, :] = f_ref[f, k]

        by_parity(lev_even, phase, send_lev)

    def blank_lev(high):
        def column(c, carry):
            for j in range(H):
                qe[(H + L if high else 0) + j, H + c] = zero
            for j in range(E):
                le[(E + L if high else 0) + j, E + c] = zero
            for j in range(W):
                for f in range(NF):
                    fe[f, (W + L if high else 0) + j, W + c] = zero_row
            return carry

        lax.fori_loop(0, C, column, 0)
        for j in range(E):
            for i in range(E):
                for col in (H - E + i, H + C + i):
                    qe[(H + L if high else H - E) + j, col] = zero
                for f in range(NF):
                    for col in (W - E + i, W + C + i):
                        fe[f, (W + L if high else W - E) + j, col] = zero_row

    for phase in range(n_lev, 2):
        by_parity(lev_even, phase, blank_lev)


def inner_body(dims, n_lev, *refs):
    T, L, C, Y = dims
    lev_in = refs[:n_lev]
    de = refs[n_lev + 3]
    qe, le, fe, me, yu, yd, yc, vu, vd, vc = refs[n_lev + 4 :]
    _, lev_even = parities()
    zero = jnp.zeros((T, Y), jnp.float32)

    for phase, source in enumerate(lev_in):

        def place_lev(high, source=source):
            q0 = H + L if high else 0
            l0 = E + L if high else 0
            f0 = W + L if high else 0

            def column(c, carry):
                rows = pl.ds(pl.multiple_of(c * T, 8), T)
                for j in range(H):
                    qe[q0 + j, H + c] = source[j, rows, :]
                for j in range(E):
                    le[l0 + j, E + c] = source[H + j, rows, :]
                return carry

            lax.fori_loop(0, C, column, 0)
            for j in range(W):
                for f in range(NF):
                    for c in range(C):
                        r = (j * NF + f) * C + c
                        fe[f, f0 + j, W + c] = source[H + E, r : r + 1, :]

        by_parity(lev_even, phase, place_lev)

    fields = Fields(fe, de, lax.axis_index("lev") * L)
    ends = lanes(T, Y)

    def own_y(i, carry):
        k = i // (C // YC)
        c0 = (i % (C // YC)) * YC
        for j in range(YC):
            c = c0 + j
            u = qe[H + k, H + c]
            v, m, _ = fields.at(1, k, c)
            d, carried, coefs = along_values(u, v, ends)
            yu[k, c], yd[k, c] = coefs()
            yc[k, c] = carried
            me[E + k, E + c] = u + along_forward(d, carried, v, m)
        return carry

    lax.fori_loop(0, L * (C // YC), own_y, 0)

    for phase in range(2):
        if phase < n_lev:
            high = lev_even if phase == 0 else jnp.logical_not(lev_even)
            k0 = jnp.where(high, L, -E)

            def beside(i, carry, k0=k0):
                k = k0 + i // (C // YC)
                c0 = (i % (C // YC)) * YC
                for j in range(YC):
                    c = c0 + j
                    u = qe[H + k, H + c]
                    v, m, _ = fields.at(1, k, c)
                    d, carried, _ = along_values(u, v, ends)
                    me[E + k, E + c] = u + along_forward(d, carried, v, m)
                return carry

            lax.fori_loop(0, E * (C // YC), beside, 0)
        else:

            def blank(high):
                def column(c, carry):
                    for j in range(E):
                        me[(E + L if high else 0) + j, E + c] = zero
                    return carry

                lax.fori_loop(0, C, column, 0)

            by_parity(lev_even, phase, blank)

    def own_v(c, carry):
        def emit(k, value):
            me[k, E + c] = me[k, E + c] + value

        def keep(k, coefs, carried):
            k = k - E
            if -1 <= k <= L:
                vu[1 + k, c], vd[1 + k, c] = coefs()
            if 0 <= k < L:
                vc[k, c] = carried

        forward_chain(
            L + 2 * E, lambda k: qe[H - E + k, H + c], lambda k: fields.at(2, k - E, c)[:2], emit, keep
        )
        return carry

    lax.fori_loop(0, C, own_v, 0)


def corner_body(dims, n_tile, *refs):
    L = dims[1]
    tile_in, lev_out = refs[:n_tile], refs[n_tile + 1 :]
    _, lev_even = parities()
    for phase, out in enumerate(lev_out):

        def send(high, out=out):
            for t in range(n_tile):
                for j in range(E):
                    out[t, j] = tile_in[t][(L - E if high else 0) + j]

        by_parity(lev_even, phase, send)


def beside_body(dims, n_tile, *refs):
    T, L, C, Y = dims
    tile_in = refs[:n_tile]
    qe, le, fe, de, me = refs[n_tile + 5 :]
    tile_even, _ = parities()
    zero = jnp.zeros((T, Y), jnp.float32)
    zero_row = jnp.zeros((1, Y), jnp.float32)

    def place_tile(source, high):
        q0 = H + C if high else 0
        l0 = E + C if high else 0
        f0 = W + C if high else 0

        def level(k, carry):
            for j in range(H):
                qe[H + k, q0 + j] = zero if source is None else source[k, j * T : (j + 1) * T, :]
            for j in range(E):
                le[E + k, l0 + j] = zero if source is None else source[k, (H + j) * T : (H + j + 1) * T, :]
            base = (H + E) * T
            for f in range(NF):
                for j in range(W):
                    r = base + W * f + j
                    fe[f, W + k, f0 + j] = zero_row if source is None else source[k, r : r + 1, :]
            return carry

        lax.fori_loop(0, L, level, 0, unroll=4)
        base = (H + E) * T + W * NF
        for j in range(W):
            de[2, f0 + j] = zero_row if source is None else source[j, base : base + 1, :]

    for phase in range(2):
        source = tile_in[phase] if phase < n_tile else None
        by_parity(tile_even, phase, lambda high, s=source: place_tile(s, high))

    depth_rows(de, [-2, -1, C, C + 1])
    for c in range(-E, C + E + 1):
        de[0, W + c] = jnp.minimum(de[2, W + c - 1], de[2, W + c])

    fields = Fields(fe, de, lax.axis_index("lev") * L)
    ends = lanes(T, Y)

    def level_y(k, carry):
        for c in (-2, -1, C, C + 1):
            u = qe[H + k, H + c]
            v, m, _ = fields.at(1, k, c)
            d, carried, _ = along_values(u, v, ends)
            me[E + k, E + c] = u + along_forward(d, carried, v, m)
        return carry

    lax.fori_loop(0, L, level_y, 0, unroll=2)

    def level_z(k, carry):
        def emit(c, value):
            me[E + k, c] = me[E + k, c] + value

        forward_chain(
            C + 2 * E, lambda c: qe[H + k, H - E + c], lambda c: fields.at(0, k, c - E)[:2], emit
        )
        return carry

    lax.fori_loop(0, L, level_z, 0)


def late_body(dims, n_tile, n_lev, *refs):
    T, L, C, Y = dims
    corner_in = refs[:n_lev]
    le, de = refs[n_lev : n_lev + 2]
    qe, fe, me, mc_ref, sp_ref = refs[n_lev + 5 : n_lev + 10]
    tile_out = refs[n_lev + 10 : n_lev + 10 + n_tile]
    lev_out = refs[n_lev + 10 + n_tile :]
    tile_even, lev_even = parities()
    zero = jnp.zeros((T, Y), jnp.float32)
    zero_row = jnp.zeros((1, Y), jnp.float32)

    def place_corner(source, tile_high, lev_high):
        for j in range(E):
            q_lev = H + L + j if lev_high else H - E + j
            f_lev = W + L + j if lev_high else W - E + j
            for i in range(E):
                s = i if tile_high else H - E + i
                col = (H + C + i) if tile_high else (H - E + i)
                qe[q_lev, col] = zero if source is None else source[j, s * T : (s + 1) * T, :]
                for f in range(NF):
                    r = (H + E) * T + W * f + (i if tile_high else W - E + i)
                    col = (W + C + i) if tile_high else (W - E + i)
                    fe[f, f_lev, col] = zero_row if source is None else source[j, r : r + 1, :]

    for phase in range(n_lev):
        for other in range(2):

            def corner(lev_high, p=phase, t=other):
                source = corner_in[p].at[t] if t < n_tile else None
                by_parity(tile_even, t, lambda tile_high: place_corner(source, tile_high, lev_high))

            by_parity(lev_even, phase, corner)

    fields = Fields(fe, de, lax.axis_index("lev") * L)

    for phase in range(n_lev):
        high = lev_even if phase == 0 else jnp.logical_not(lev_even)
        k0 = jnp.where(high, L, -E)

        def beside(j, carry, k0=k0):
            k = k0 + j

            def emit(c, value):
                me[E + k, E + c] = me[E + k, E + c] + value

            forward_chain(C, lambda c: qe[H + k, H + c], lambda c: fields.at(0, k, c)[:2], emit)
            return carry

        lax.fori_loop(0, E, beside, 0)

    def side_v(i, carry):
        c = jnp.where(i < E, i - E, C - E + i)

        def emit(k, value):
            me[E + k, E + c] = me[E + k, E + c] + value

        forward_chain(L, lambda k: qe[H + k, H + c], lambda k: fields.at(2, k, c)[:2], emit)
        return carry

    lax.fori_loop(0, 2 * E, side_v, 0)

    def done(k, c, value):
        mc_ref[k, c] = value

    adjoint(dims, fields, me, E, le, mc_ref, done, sp_ref)

    for phase, out in enumerate(tile_out):

        def send_tile(high, out=out):
            def level(k, carry):
                for j in range(E):
                    out[k, j] = mc_ref[k, (C - E if high else 0) + j]
                return carry

            lax.fori_loop(0, L, level, 0)

        by_parity(tile_even, phase, send_tile)
    for phase, out in enumerate(lev_out):

        def send_lev(high, out=out):
            def column(c, carry):
                for j in range(E):
                    out[j, c] = mc_ref[(L - E if high else 0) + j, c]
                return carry

            lax.fori_loop(0, C, column, 0)

        by_parity(lev_even, phase, send_lev)


def adjoint(dims, fields, u_ref, uo, l_ref, acc_ref, done, speed_ref, kept=None):
    T, L, C, Y = dims
    ends = lanes(T, Y)
    yu, yd, yc, vu, vd, vc = kept or [None] * 6

    def store_speed(direction, k, c, is_open, value):
        row = jnp.sum(value, axis=0, keepdims=True)
        speed_ref[direction, k, pl.ds(c, 1), :] = jnp.where(is_open, row, 0.0)

    def along(i, carry):
        k = i // (C // YC)
        c0 = (i % (C // YC)) * YC
        for j in range(YC):
            c = c0 + j
            l = l_ref[E + k, E + c]
            v, m, is_open = fields.at(1, k, c)
            if kept is None:
                _, carried, coefs = along_values(u_ref[uo + k, uo + c], v, ends)
                up, down = coefs()
            else:
                up, down, carried = yu[k, c], yd[k, c], yc[k, c]
            add, g = along_adjoint(l, v, m, up, down, ends)
            acc_ref[k, c] = l + add
            store_speed(1, k, c, is_open, g * carried)
        return carry

    lax.fori_loop(0, L * (C // YC), along, 0)

    def level_z(k, carry):
        opened = {}

        def co(c):
            v, m, opened[c] = fields.at(0, k, c)
            return v, m

        def emit(c, value):
            acc_ref[k, c] = acc_ref[k, c] + value

        adjoint_chain(
            C,
            fresh_limits(lambda c: u_ref[uo + k, uo + c]),
            lambda c: l_ref[E + k, E + c],
            co,
            emit,
            lambda c, value: store_speed(0, k, c, opened[c], value),
        )
        return carry

    lax.fori_loop(0, L, level_z, 0)

    def column_v(c, carry):
        opened = {}

        def co(k):
            v, m, opened[k] = fields.at(2, k, c)
            return v, m

        def emit(k, value):
            done(k, c, acc_ref[k, c] + value)

        if kept is None:
            limits = fresh_limits(lambda k: u_ref[uo + k, uo + c])
        else:

            def limits(f, v):
                k = f - 1
                return vu[1 + k, c], vd[1 + k, c], vc[k, c] if 0 <= k < L else None

        adjoint_chain(
            L,
            limits,
            lambda k: l_ref[E + k, E + c],
            co,
            emit,
            lambda k, value: store_speed(2, k, c, opened[k], value),
        )
        return carry

    lax.fori_loop(0, C, column_v, 0)


def start_body(dims, n_tile, n_lev, *refs):
    T, L, C, Y = dims
    qe, fe, de, mc_ref, late_ref = refs[:5]
    kept = refs[5:11]
    tile_in = refs[11 : 11 + n_tile]
    lev_in = refs[11 + n_tile : 11 + n_tile + n_lev]
    out_ref, sp_out, *rest = refs[11 + n_tile + n_lev :]
    given_ref = rest[0] if len(rest) == 4 else None
    le, acc, sp_ref = rest[-3:]
    tile_even, lev_even = parities()
    zero = jnp.zeros((T, Y), jnp.float32)

    def own(k, carry):
        for c in range(C):
            le[E + k, E + c] = mc_ref[k, c]
        return carry

    lax.fori_loop(0, L, own, 0)

    def place_tile(source, high):
        def level(k, carry):
            for j in range(E):
                le[E + k, (E + C if high else 0) + j] = zero if source is None else source[k, j]
            return carry

        lax.fori_loop(0, L, level, 0)

    def place_lev(source, high):
        def column(c, carry):
            for j in range(E):
                le[(E + L if high else 0) + j, E + c] = zero if source is None else source[j, c]
            return carry

        lax.fori_loop(0, C, column, 0)

    for phase in range(2):
        by_parity(
            tile_even, phase, lambda high, p=phase: place_tile(tile_in[p] if p < n_tile else None, high)
        )
        by_parity(lev_even, phase, lambda high, p=phase: place_lev(lev_in[p] if p < n_lev else None, high))

    def done(k, c, value):
        out_ref[pl.ds(k * C + c, T, stride=L * C), :] = value

    adjoint(dims, Fields(fe, de, lax.axis_index("lev") * L), qe, H, le, acc, done, sp_ref, kept)
    if given_ref is None:
        sp_out[...] = sp_ref[...] + late_ref[...]
        return
    half = L // 2
    low = lax.axis_index("trc") == 0
    for keeps_low in (True, False):

        @pl.when(low if keeps_low else jnp.logical_not(low))
        def _(keeps_low=keeps_low):
            for out, first in ((sp_out, keeps_low), (given_ref, not keeps_low)):
                k0 = 0 if first else half
                out[...] = sp_ref[:, k0 : k0 + half] + late_ref[:, k0 : k0 + half]


def f32(*shape):
    return jax.ShapeDtypeStruct(shape, jnp.float32)


def call(body, outs, scratch, args, hbm=0, aliases=None, mib=4):
    return run(body, outs, scratch, args, hbm, aliases, mib)


def run(body, outs, scratch, args, hbm, aliases, mib):
    vmem = pl.BlockSpec(memory_space=pltpu.VMEM)
    return pl.pallas_call(
        body,
        out_shape=outs,
        in_specs=[pl.BlockSpec(memory_space=pltpu.HBM)] * hbm + [vmem] * (len(args) - hbm),
        out_specs=[vmem] * len(outs),
        scratch_shapes=scratch,
        input_output_aliases=aliases or {},
        compiler_params=pltpu.CompilerParams(vmem_limit_bytes=mib * 1024 * 1024),
    )(*args)


def swap(values, axis, pairings_):
    received = []
    for x, pairs in zip(values, pairings_):
        received.append(lax.ppermute(x, axis, pairs))
    return received


def program(tracers, cotangent, zonal_speed, meridional_speed, vertical_speed, lateral_mixing, vertical_mixing, column_depth):
    dims = T, L, C, Y = tracers.shape
    tile_pairs = pairings(lax.axis_size("tile"))
    lev_pairs = pairings(lax.axis_size("lev"))
    n_tile, n_lev = len(tile_pairs), len(lev_pairs)
    q = tracers.reshape(T * L * C, Y)
    l = cotangent.reshape(T * L * C, Y)
    inputs = [q, l, zonal_speed, meridional_speed, vertical_speed, lateral_mixing, vertical_mixing, column_depth]
    landing = [
        pltpu.VMEM((T * L * C, Y), jnp.float32),
        pltpu.VMEM((T * L * C, Y), jnp.float32),
        pltpu.VMEM((NF, L, C, Y), jnp.float32),
        pltpu.VMEM((C, Y), jnp.int32),
        pltpu.SemaphoreType.DMA((8,)),
    ]

    tile_rows = (H + E) * T + FPAD
    lev_rows = max(C * T, W * NF * C)
    to_tile = call(
        functools.partial(edges_body, dims, n_tile), [f32(L, tile_rows, Y)] * n_tile, landing, inputs, hbm=8, mib=MIB
    )
    from_tile = swap(to_tile, "tile", tile_pairs)

    qe_s = f32(L + 2 * H, C + 2 * H, T, Y)
    ext_s = f32(L + 2 * E, C + 2 * E, T, Y)
    fe_s = f32(NF, L + 2 * W, C + 2 * W, 1, Y)
    de_s = f32(3, C + 2 * W, 1, Y)
    own_s = f32(L, C, T, Y)
    *to_lev, qe, le, fe, de = call(
        functools.partial(own_body, dims, n_lev),
        [f32(H + E + 1, lev_rows, Y)] * n_lev + [qe_s, ext_s, fe_s, de_s],
        landing,
        inputs + [to_tile[0]],
        hbm=8,
    )
    from_lev = swap(to_lev, "lev", lev_pairs)
    n = n_lev
    qe, le, fe, me, *kept = call(
        functools.partial(inner_body, dims, n_lev),
        [qe_s, ext_s, fe_s, ext_s] + [own_s] * 3 + [f32(L + 2, C, T, Y)] * 2 + [own_s],
        [],
        [*from_lev, qe, le, fe, de],
        aliases={n: 0, n + 1: 1, n + 2: 2},
    )
    to_lev = call(
        functools.partial(corner_body, dims, n_tile), [f32(n_tile, E, tile_rows, Y)] * n_lev, [], [*from_tile, me]
    )
    corners = swap(to_lev, "lev", lev_pairs)
    n = n_tile
    qe, le, fe, de, me = call(
        functools.partial(beside_body, dims, n_tile),
        [qe_s, ext_s, fe_s, de_s, ext_s],
        [],
        [*from_tile, qe, le, fe, de, me],
        aliases={n + i: i for i in range(5)},
    )
    n = n_lev
    qe, fe, me, mc, late, *mc_edges = call(
        functools.partial(late_body, dims, n_tile, n_lev),
        [qe_s, fe_s, ext_s, own_s, f32(3, L, C, Y)] + [f32(L, E, T, Y)] * n_tile + [f32(E, C, T, Y)] * n_lev,
        [],
        [*corners, le, de, qe, fe, me],
        aliases={n + 2: 0, n + 3: 1, n + 4: 2},
    )
    mc_tile = swap(mc_edges[:n_tile], "tile", tile_pairs)
    mc_lev = swap(mc_edges[n_tile:], "lev", lev_pairs)
    pair = lax.axis_size("trc") == 2 and L % 2 == 0
    start, speeds, *given = call(
        functools.partial(start_body, dims, n_tile, n_lev),
        [f32(T * L * C, Y)] + ([f32(3, L // 2, C, Y)] * 2 if pair else [f32(3, L, C, Y)]),
        [pltpu.VMEM(x.shape, jnp.float32) for x in (ext_s, own_s, f32(3, L, C, Y))],
        [qe, fe, de, mc, late, *kept, *mc_tile, *mc_lev],
    )
    if pair:
        speeds = speeds + lax.ppermute(given[0], "trc", [(0, 1), (1, 0)])
    else:
        speeds = lax.psum_scatter(speeds, "trc", scatter_dimension=1, tiled=True)
    return start.reshape(T, L, C, Y), speeds


def solution(mesh):
    return jax.shard_map(
        program,
        mesh=mesh,
        in_specs=(
            P("trc", "lev", ("ens", "tile"), None),
            P("trc", "lev", ("ens", "tile"), None),
            P("lev", ("ens", "tile"), None),
            P("lev", ("ens", "tile"), None),
            P("lev", ("ens", "tile"), None),
            P("lev", ("ens", "tile"), None),
            P("lev", ("ens", "tile"), None),
            P(("ens", "tile"), None),
        ),
        out_specs=(
            P("trc", "lev", ("ens", "tile"), None),
            P(None, ("lev", "trc"), ("ens", "tile"), None),
        ),
        check_vma=False,
    )
```

```python
import functools

import jax
import jax.numpy as jnp
from jax import lax
from jax.experimental import pallas as pl
from jax.experimental.pallas import tpu as pltpu
from jax.sharding import PartitionSpec as P

albada_floor = 0.01
H = 4
E = 2
W = 3
NF = 5
MIB = 4
FPAD = 16


def pairings(count):
    phases = []
    for first in (0, 1):
        pairs = []
        for i in range(first, count - 1, 2):
            pairs += [(i, i + 1), (i + 1, i)]
        if pairs:
            phases.append(pairs)
    return phases


def by_parity(even, phase, act):
    @pl.when(even)
    def _():
        act(phase == 0)

    @pl.when(jnp.logical_not(even))
    def _():
        act(phase == 1)


def limiter(x, y, xx, yy):
    s = x * y
    r = 1.0 / (xx + yy + albada_floor)
    a = s * (x + y) * r
    return s, r, a


def slopes(x, y, xx, yy, s, r, a):
    return r * (0.5 * yy + s - x * a), r * (0.5 * xx + s - y * a)


def forward_chain(n, get_u, get_co, emit, keep=None):
    u_a, u_b = get_u(-2), get_u(-1)
    d_b = u_b - u_a
    xx_b = d_b * d_b
    half_b = None
    flux_b = None
    for f in range(0, n + 2):
        u_c = get_u(f)
        d_c = u_c - u_b
        xx_c = d_c * d_c
        s, r, a = limiter(d_b, d_c, xx_b, xx_c)
        half_c = 0.5 * a
        carried = None
        if f >= 1:
            v, m = get_co(f - 1)
            carried = jnp.where(v >= 0.0, u_a + half_b, u_b - half_c)
            flux = v * carried - m * d_b
            if f >= 2:
                emit(f - 2, flux_b - flux)
            flux_b = flux
        if keep is not None:
            keep(f - 1, lambda: slopes(d_b, d_c, xx_b, xx_c, s, r, a), carried)
        u_a, u_b, d_b, xx_b, half_b = u_b, u_c, d_c, xx_c, half_c


def fresh_limits(get_u):
    state = {"u_a": get_u(-2), "u_b": get_u(-1), "half": None}
    state["d"] = state["u_b"] - state["u_a"]
    state["xx"] = state["d"] * state["d"]

    def step(f, v):
        u_a, u_b, d_b, xx_b = state["u_a"], state["u_b"], state["d"], state["xx"]
        u_c = get_u(f)
        d_c = u_c - u_b
        xx_c = d_c * d_c
        s, r, a = limiter(d_b, d_c, xx_b, xx_c)
        half_c = 0.5 * a
        carried = None
        if f >= 1:
            carried = jnp.where(v >= 0.0, u_a + state["half"], u_b - half_c)
        state.update(u_a=u_b, u_b=u_c, half=half_c, d=d_c, xx=xx_c)
        up, down = slopes(d_b, d_c, xx_b, xx_c, s, r, a)
        return up, down, carried

    return step


def adjoint_chain(n, limits, get_l, get_co, emit, emit_speed):
    l_b = get_l(-1)
    g_b = l_b - get_l(-2)
    v_b, _ = get_co(-1)
    n_b = jnp.minimum(v_b, 0.0) * g_b
    p_b = dm_b = down_a = dd_a = n_a = None
    for f in range(0, n + 2):
        l_c = get_l(f)
        g_c = l_c - l_b
        v_c, m_c = get_co(f)
        p_c = jnp.maximum(v_c, 0.0) * g_c
        n_c = jnp.minimum(v_c, 0.0) * g_c
        up, down, carried = limits(f, v_b)
        e = p_c - n_b
        if f >= 1:
            dd_b = e * up + down_a - dm_b
            if f >= 2:
                emit(f - 2, n_a + p_b + dd_a - dd_b)
            if emit_speed is not None and f - 1 < n:
                emit_speed(f - 1, g_b * carried)
            dd_a = dd_b
        down_a = e * down
        n_a = n_b
        p_b, n_b, v_b = p_c, n_c, v_c
        dm_b = m_c * g_c
        g_b, l_b = g_c, l_c


def lanes(T, Y):
    lane = lax.broadcasted_iota(jnp.int32, (T, Y), 1)
    return lane == 0, lane == Y - 1


def along_values(u, v, ends):
    first, last = ends
    Y = u.shape[-1]
    before = jnp.where(first, 0.0, pltpu.roll(u, 1, 1))
    d = u - before
    nxt = jnp.where(last, -u, pltpu.roll(d, Y - 1, 1))
    xx, yy = d * d, nxt * nxt
    s, r, a = limiter(d, nxt, xx, yy)
    half = 0.5 * a
    carried = jnp.where(v >= 0.0, before + pltpu.roll(half, 1, 1), u - half)
    return d, carried, lambda: slopes(d, nxt, xx, yy, s, r, a)


def along_forward(d, carried, v, m):
    flux = v * carried - m * d
    return flux - pltpu.roll(flux, flux.shape[-1] - 1, 1)


def along_adjoint(l, v, m, up, down, ends):
    first, last = ends
    Y = l.shape[-1]
    g = l - pltpu.roll(l, 1, 1)
    p = jnp.maximum(v, 0.0) * g
    n = jnp.minimum(v, 0.0) * g
    e = pltpu.roll(p, Y - 1, 1) - n
    z = e * up - m * g
    y = e * down
    add = (
        (n + z - y)
        + jnp.where(first, 0.0, pltpu.roll(y, 1, 1))
        + jnp.where(last, 0.0, pltpu.roll(p - z, Y - 1, 1))
    )
    return add, g


class Fields:
    def __init__(self, f_ref, d_ref, level0):
        self.f, self.d, self.level0 = f_ref, d_ref, level0

    def open(self, direction, k, c):
        level = (self.level0 + k).astype(jnp.float32)
        if direction == 2:
            level = jnp.where(level >= 1.0, level, 1e9)
        return self.d[direction, W + c] > level

    def at(self, direction, k, c):
        is_open = self.open(direction, k, c)
        speed = self.f[direction, W + k, W + c]
        mix = self.f[(3, 3, 4)[direction], W + k, W + c]
        return jnp.where(is_open, speed, 0.0), jnp.where(is_open, mix, 0.0), is_open


def parities():
    return lax.axis_index("tile") % 2 == 0, lax.axis_index("lev") % 2 == 0


def depth_rows(de, columns):
    Y = de.shape[-1]
    lane0 = lax.broadcasted_iota(jnp.int32, (1, Y), 1) == 0
    for c in columns:
        here = de[2, W + c]
        de[1, W + c] = jnp.where(lane0, 0.0, jnp.minimum(pltpu.roll(here, 1, 1), here))


def edges_body(dims, n_tile, *refs):
    T, L, C, _ = dims
    sources, tile_out, (q_ref, l_ref, f_ref, d_ref, sem) = refs[:8], refs[8 : 8 + n_tile], refs[8 + n_tile :]
    targets = [q_ref, l_ref] + [f_ref.at[f] for f in range(NF)] + [d_ref]
    order = [0] + list(range(2, 8)) + [1]
    copies = [pltpu.make_async_copy(sources[i], targets[i], sem.at[i]) for i in order]
    for c in copies:
        c.start()
    for c in copies[1:-1] + copies[:1]:
        c.wait()
    tile_even, _ = parities()

    for phase, out in enumerate(tile_out):

        def send_tile(high, out=out):
            q0 = C - H if high else 0
            f0 = C - W if high else 0

            def level(k, carry):
                for j in range(H):
                    out[k, j * T : (j + 1) * T, :] = q_ref[pl.ds(k * C + q0 + j, T, stride=L * C), :]
                for f in range(NF):
                    r = H * T + W * f
                    out[k, r : r + W, :] = f_ref[f, k, f0 : f0 + W, :]
                r = H * T + W * NF
                out[k, r : r + 1, :] = d_ref[f0 : f0 + 1, :].astype(jnp.float32)
                return carry

            lax.fori_loop(0, L, level, 0, unroll=2)
            r = H * T + W * NF
            for j in range(1, W):
                out[j, r : r + 1, :] = d_ref[f0 + j : f0 + j + 1, :].astype(jnp.float32)

        by_parity(tile_even, phase, send_tile)
    copies[-1].wait()


def own_body(dims, n_tile, n_lev, *refs):
    T, L, C, Y = dims
    q_ref, l_ref, f_ref, d_ref = refs[:4]
    tile_out, lev_out = refs[4 : 4 + n_tile], refs[4 + n_tile : 4 + n_tile + n_lev]
    qe, le, fe, de = refs[4 + n_tile + n_lev :]
    tile_even, lev_even = parities()
    zero = jnp.zeros((T, Y), jnp.float32)
    zero_row = jnp.zeros((1, Y), jnp.float32)

    def own_level(k, carry):
        for c in range(C):
            qe[H + k, H + c] = q_ref[pl.ds(k * C + c, T, stride=L * C), :]
            le[E + k, E + c] = l_ref[pl.ds(k * C + c, T, stride=L * C), :]
            for f in range(NF):
                fe[f, W + k, W + c] = f_ref[f, k, c : c + 1, :]
        return carry

    lax.fori_loop(0, L, own_level, 0)
    for c in range(C):
        de[2, W + c] = d_ref[c : c + 1, :].astype(jnp.float32)
    depth_rows(de, range(C))

    for phase, out in enumerate(tile_out):

        def send_tile(high, out=out):
            def level(k, carry):
                for j in range(E):
                    out[k, j] = le[E + k, E + (C - E if high else 0) + j]
                return carry

            lax.fori_loop(0, L, level, 0, unroll=2)

        by_parity(tile_even, phase, send_tile)

    for phase, out in enumerate(lev_out):

        def send_lev(high, out=out):
            def column(c, carry):
                rows = pl.ds(pl.multiple_of(c * T, 8), T)
                for j in range(H):
                    out[j, rows, :] = qe[H + (L - H if high else 0) + j, H + c]
                for j in range(E):
                    out[H + j, rows, :] = le[E + (L - E if high else 0) + j, E + c]
                return carry

            lax.fori_loop(0, C, column, 0)
            for j in range(W):
                k = (L - W if high else 0) + j
                for f in range(NF):
                    out[H + E, (j * NF + f) * C : (j * NF + f + 1) * C, :] = f_ref[f, k]

        by_parity(lev_even, phase, send_lev)

    def blank_lev(high):
        def column(c, carry):
            for j in range(H):
                qe[(H + L if high else 0) + j, H + c] = zero
            for j in range(E):
                le[(E + L if high else 0) + j, E + c] = zero
            for j in range(W):
                for f in range(NF):
                    fe[f, (W + L if high else 0) + j, W + c] = zero_row
            return carry

        lax.fori_loop(0, C, column, 0)
        for j in range(E):
            for i in range(E):
                for col in (H - E + i, H + C + i):
                    qe[(H + L if high else H - E) + j, col] = zero
                for f in range(NF):
                    for col in (W - E + i, W + C + i):
                        fe[f, (W + L if high else W - E) + j, col] = zero_row

    for phase in range(n_lev, 2):
        by_parity(lev_even, phase, blank_lev)


def inner_y_body(dims, qe, fe, de, me, yu, yd, yc):
    T, L, C, Y = dims
    fields = Fields(fe, de, lax.axis_index("lev") * L)
    ends = lanes(T, Y)

    def own_y(k, carry):
        for c in range(C):
            u = qe[H + k, H + c]
            v, m, _ = fields.at(1, k, c)
            d, carried, coefs = along_values(u, v, ends)
            yu[k, c], yd[k, c] = coefs()
            yc[k, c] = carried
            me[E + k, E + c] = u + along_forward(d, carried, v, m)
        return carry

    lax.fori_loop(0, L, own_y, 0)


def inner_v_body(dims, n_lev, *refs):
    T, L, C, Y = dims
    lev_in = refs[:n_lev]
    de = refs[n_lev + 4]
    qe, le, fe, me, vu, vd, vc = refs[n_lev + 5 :]
    _, lev_even = parities()
    zero = jnp.zeros((T, Y), jnp.float32)

    for phase, source in enumerate(lev_in):

        def place_lev(high, source=source):
            q0 = H + L if high else 0
            l0 = E + L if high else 0
            f0 = W + L if high else 0

            def column(c, carry):
                rows = pl.ds(pl.multiple_of(c * T, 8), T)
                for j in range(H):
                    qe[q0 + j, H + c] = source[j, rows, :]
                for j in range(E):
                    le[l0 + j, E + c] = source[H + j, rows, :]
                return carry

            lax.fori_loop(0, C, column, 0)
            for j in range(W):
                for f in range(NF):
                    for c in range(C):
                        r = (j * NF + f) * C + c
                        fe[f, f0 + j, W + c] = source[H + E, r : r + 1, :]

        by_parity(lev_even, phase, place_lev)

    fields = Fields(fe, de, lax.axis_index("lev") * L)
    ends = lanes(T, Y)

    for phase in range(2):
        if phase < n_lev:
            high = lev_even if phase == 0 else jnp.logical_not(lev_even)
            k0 = jnp.where(high, L, -E)

            def beside(i, carry, k0=k0):
                k = k0 + i
                for c in range(C):
                    u = qe[H + k, H + c]
                    v, m, _ = fields.at(1, k, c)
                    d, carried, _ = along_values(u, v, ends)
                    me[E + k, E + c] = u + along_forward(d, carried, v, m)
                return carry

            lax.fori_loop(0, E, beside, 0)
        else:

            def blank(high):
                def column(c, carry):
                    for j in range(E):
                        me[(E + L if high else 0) + j, E + c] = zero
                    return carry

                lax.fori_loop(0, C, column, 0)

            by_parity(lev_even, phase, blank)

    def own_v(c, carry):
        def emit(k, value):
            me[k, E + c] = me[k, E + c] + value

        def keep(k, coefs, carried):
            k = k - E
            if -1 <= k <= L:
                vu[1 + k, c], vd[1 + k, c] = coefs()
            if 0 <= k < L:
                vc[k, c] = carried

        forward_chain(
            L + 2 * E, lambda k: qe[H - E + k, H + c], lambda k: fields.at(2, k - E, c)[:2], emit, keep
        )
        return carry

    lax.fori_loop(0, C, own_v, 0)


def corner_body(dims, n_tile, *refs):
    L = dims[1]
    tile_in, lev_out = refs[:n_tile], refs[n_tile + 1 :]
    _, lev_even = parities()
    for phase, out in enumerate(lev_out):

        def send(high, out=out):
            for t in range(n_tile):
                for j in range(E):
                    out[t, j] = tile_in[t][(L - E if high else 0) + j]

        by_parity(lev_even, phase, send)


def beside_body(dims, n_tile, *refs):
    T, L, C, Y = dims
    tile_in = refs[:n_tile]
    qe, fe, de, me, zc = refs[n_tile + 4 :]
    tile_even, _ = parities()
    zero = jnp.zeros((T, Y), jnp.float32)
    zero_row = jnp.zeros((1, Y), jnp.float32)

    def place_tile(source, high):
        q0 = H + C if high else 0
        f0 = W + C if high else 0

        def level(k, carry):
            for j in range(H):
                qe[H + k, q0 + j] = zero if source is None else source[k, j * T : (j + 1) * T, :]
            base = H * T
            for f in range(NF):
                for j in range(W):
                    r = base + W * f + j
                    fe[f, W + k, f0 + j] = zero_row if source is None else source[k, r : r + 1, :]
            return carry

        lax.fori_loop(0, L, level, 0, unroll=4)
        base = H * T + W * NF
        for j in range(W):
            de[2, f0 + j] = zero_row if source is None else source[j, base : base + 1, :]

    for phase in range(2):
        source = tile_in[phase] if phase < n_tile else None
        by_parity(tile_even, phase, lambda high, s=source: place_tile(s, high))

    depth_rows(de, [-2, -1, C, C + 1])
    for c in range(-E, C + E + 1):
        de[0, W + c] = jnp.minimum(de[2, W + c - 1], de[2, W + c])

    fields = Fields(fe, de, lax.axis_index("lev") * L)
    ends = lanes(T, Y)

    def level_y(k, carry):
        for c in (-2, -1, C, C + 1):
            u = qe[H + k, H + c]
            v, m, _ = fields.at(1, k, c)
            d, carried, _ = along_values(u, v, ends)
            me[E + k, E + c] = u + along_forward(d, carried, v, m)
        return carry

    lax.fori_loop(0, L, level_y, 0, unroll=2)

    def level_z(k, carry):
        def emit(c, value):
            me[E + k, c] = me[E + k, c] + value

        def keep(c, coefs, carried):
            if 0 <= c - E < C:
                zc[k, c - E] = carried

        forward_chain(
            C + 2 * E, lambda c: qe[H + k, H - E + c], lambda c: fields.at(0, k, c - E)[:2], emit, keep
        )
        return carry

    lax.fori_loop(0, L, level_z, 0)


def late_body(dims, n_tile, n_lev, *refs):
    T, L, C, Y = dims
    corner_in, tile_in = refs[:n_lev], refs[n_lev : n_lev + n_tile]
    de = refs[n_lev + n_tile]
    qe, le, fe, me, mc_ref, sp_ref, *tile_out = refs[n_lev + n_tile + 5 :]
    tile_even, lev_even = parities()
    zero = jnp.zeros((T, Y), jnp.float32)
    zero_row = jnp.zeros((1, Y), jnp.float32)

    def place_corner(source, tile_high, lev_high):
        for j in range(E):
            q_lev = H + L + j if lev_high else H - E + j
            f_lev = W + L + j if lev_high else W - E + j
            for i in range(E):
                s = i if tile_high else H - E + i
                col = (H + C + i) if tile_high else (H - E + i)
                qe[q_lev, col] = zero if source is None else source[j, s * T : (s + 1) * T, :]
                for f in range(NF):
                    r = H * T + W * f + (i if tile_high else W - E + i)
                    col = (W + C + i) if tile_high else (W - E + i)
                    fe[f, f_lev, col] = zero_row if source is None else source[j, r : r + 1, :]

    for phase in range(n_lev):
        for other in range(2):

            def corner(lev_high, p=phase, t=other):
                source = corner_in[p].at[t] if t < n_tile else None
                by_parity(tile_even, t, lambda tile_high: place_corner(source, tile_high, lev_high))

            by_parity(lev_even, phase, corner)

    def place_tile(source, high):
        def level(k, carry):
            for j in range(E):
                le[E + k, (E + C if high else 0) + j] = zero if source is None else source[k, j]
            return carry

        lax.fori_loop(0, L, level, 0, unroll=2)

    for phase in range(2):
        source = tile_in[phase] if phase < n_tile else None
        by_parity(tile_even, phase, lambda high, s=source: place_tile(s, high))

    fields = Fields(fe, de, lax.axis_index("lev") * L)

    for phase in range(n_lev):
        high = lev_even if phase == 0 else jnp.logical_not(lev_even)
        k0 = jnp.where(high, L, -E)

        def beside(j, carry, k0=k0):
            k = k0 + j

            def emit(c, value):
                me[E + k, E + c] = me[E + k, E + c] + value

            forward_chain(C, lambda c: qe[H + k, H + c], lambda c: fields.at(0, k, c)[:2], emit)
            return carry

        lax.fori_loop(0, E, beside, 0)

    def side_v(i, carry):
        c = jnp.where(i < E, i - E, C - E + i)

        def emit(k, value):
            me[E + k, E + c] = me[E + k, E + c] + value

        forward_chain(L, lambda k: qe[H + k, H + c], lambda k: fields.at(2, k, c)[:2], emit)
        return carry

    lax.fori_loop(0, 2 * E, side_v, 0)

    def done(k, c, value):
        mc_ref[k, c] = value

    adjoint(dims, fields, me, E, le, mc_ref, done, parts(C)[0], sp_ref)

    for phase, out in enumerate(tile_out):

        def send_tile(high, out=out):
            def level(k, carry):
                for j in range(E):
                    out[k, j] = mc_ref[k, (C - E if high else 0) + j]
                return carry

            lax.fori_loop(0, L, level, 0, unroll=2)

        by_parity(tile_even, phase, send_tile)


def late_inner_body(dims, *refs):
    _, L, C, _ = dims
    le, fe, de, me = refs[:4]
    mc_ref, sp_ref, *lev_out = refs[6:]
    _, lev_even = parities()

    def done(k, c, value):
        mc_ref[k, c] = value

    fields = Fields(fe, de, lax.axis_index("lev") * L)
    adjoint(dims, fields, me, E, le, mc_ref, done, parts(C)[1], sp_ref)

    for phase, out in enumerate(lev_out):

        def send_lev(high, out=out):
            def column(c, carry):
                for j in range(E):
                    out[j, c] = mc_ref[(L - E if high else 0) + j, c]
                return carry

            lax.fori_loop(0, C, column, 0, unroll=2)

        by_parity(lev_even, phase, send_lev)


def parts(C):
    edge = (list(range(E)) + list(range(C - E, C)), [(0, E), (C - E, E)], lambda i: jnp.where(i < E, i, C - 2 * E + i))
    inner = (list(range(E, C - E)), [(E, C - 2 * E)] if C > 2 * E else [], lambda i: E + i)
    return edge, inner


def adjoint(dims, fields, u_ref, uo, l_ref, acc_ref, done, part, speed_ref=None, kept=None, passes="yzv"):
    T, L, _, Y = dims
    ends = lanes(T, Y)
    yu, yd, vu, vd = kept or [None] * 4
    columns, runs, column_of = part

    def store_speed(direction, k, c, is_open, value):
        if speed_ref is not None:
            row = jnp.sum(value, axis=0, keepdims=True)
            speed_ref[direction, k, pl.ds(c, 1), :] = jnp.where(is_open, row, 0.0)

    def along(k, carry):
        for c in columns:
            l = l_ref[E + k, E + c]
            v, m, is_open = fields.at(1, k, c)
            if kept is None:
                _, carried, coefs = along_values(u_ref[uo + k, uo + c], v, ends)
                up, down = coefs()
            else:
                up, down = yu[k, c], yd[k, c]
            add, g = along_adjoint(l, v, m, up, down, ends)
            acc_ref[k, c] = l + add
            if speed_ref is not None:
                store_speed(1, k, c, is_open, g * carried)
        return carry

    if "y" in passes:
        lax.fori_loop(0, L, along, 0, unroll=2)

    def level_z(k, carry):
        for c0, n in runs:
            opened = {}

            def co(c, c0=c0, opened=opened):
                v, m, opened[c] = fields.at(0, k, c0 + c)
                return v, m

            def emit(c, value, c0=c0):
                acc_ref[k, c0 + c] = acc_ref[k, c0 + c] + value

            def speed(c, value, c0=c0, opened=opened):
                store_speed(0, k, c0 + c, opened[c], value)

            adjoint_chain(
                n,
                fresh_limits(lambda c, c0=c0: u_ref[uo + k, uo + c0 + c]),
                lambda c, c0=c0: l_ref[E + k, E + c0 + c],
                co,
                emit,
                speed if speed_ref is not None else None,
            )
        return carry

    if "z" in passes:
        lax.fori_loop(0, L, level_z, 0)

    def column_v(i, carry):
        c = column_of(i)
        opened = {}

        def co(k):
            v, m, opened[k] = fields.at(2, k, c)
            return v, m

        def emit(k, value):
            done(k, c, acc_ref[k, c] + value)

        if kept is None:
            limits = fresh_limits(lambda k: u_ref[uo + k, uo + c])
        else:

            def limits(f, v):
                return vu[f, c], vd[f, c], None

        adjoint_chain(
            L,
            limits,
            lambda k: l_ref[E + k, E + c],
            co,
            emit,
            (lambda k, value: store_speed(2, k, c, opened[k], value)) if speed_ref is not None else None,
        )
        return carry

    if "v" in passes:
        lax.fori_loop(0, len(columns), column_v, 0)


def start_inner_body(dims, *refs):
    _, L, C, _ = dims
    qe, fe, de, mc_ref, yu, yd, le, acc = refs

    def own(k, carry):
        for c in range(C):
            le[E + k, E + c] = mc_ref[k, c]
        return carry

    lax.fori_loop(0, L, own, 0, unroll=2)
    fields = Fields(fe, de, lax.axis_index("lev") * L)
    adjoint(dims, fields, qe, H, le, acc, None, parts(C)[1], kept=(yu, yd, None, None), passes="yz")


def start_levels_body(dims, n_lev, *refs):
    T, L, C, Y = dims
    fe, de, vu, vd, acc = refs[:5]
    lev_in = refs[5 : 5 + n_lev]
    le, out_ref = refs[6 + n_lev :]
    _, lev_even = parities()
    zero = jnp.zeros((T, Y), jnp.float32)

    def place_lev(source, high):
        def column(c, carry):
            for j in range(E):
                le[(E + L if high else 0) + j, E + c] = zero if source is None else source[j, c]
            return carry

        lax.fori_loop(0, C, column, 0, unroll=2)

    for phase in range(2):
        source = lev_in[phase] if phase < n_lev else None
        by_parity(lev_even, phase, lambda high, s=source: place_lev(s, high))

    def done(k, c, value):
        out_ref[pl.ds(k * C + c, T, stride=L * C), :] = value

    fields = Fields(fe, de, lax.axis_index("lev") * L)
    adjoint(dims, fields, None, H, le, acc, done, parts(C)[1], kept=(None, None, vu, vd), passes="v")


def speeds_body(dims, n_tile, *refs):
    T, L, C, Y = dims
    fe, de, late_ref, zc, yc, vc = refs[:6]
    tile_in = refs[6 : 6 + n_tile]
    le, *outs, sp_ref = refs[7 + n_tile :]
    tile_even, _ = parities()
    zero = jnp.zeros((T, Y), jnp.float32)

    def place_tile(source, high):
        def level(k, carry):
            for j in range(E):
                le[E + k, (E + C if high else 0) + j] = zero if source is None else source[k, j]
            return carry

        lax.fori_loop(0, L, level, 0, unroll=2)

    for phase in range(2):
        source = tile_in[phase] if phase < n_tile else None
        by_parity(tile_even, phase, lambda high, s=source: place_tile(s, high))

    fields = Fields(fe, de, lax.axis_index("lev") * L)

    def level(k, carry):
        for c in range(C):
            l = le[E + k, E + c]
            befores = (le[E + k, E + c - 1], pltpu.roll(l, 1, 1), le[E + k - 1, E + c])
            for direction, before, carried in zip(range(3), befores, (zc, yc, vc)):
                row = jnp.sum((l - before) * carried[k, c], axis=0, keepdims=True)
                row = jnp.where(fields.open(direction, k, c), row, 0.0)
                sp_ref[direction, k, c : c + 1, :] = row
        return carry

    lax.fori_loop(0, L, level, 0)
    if len(outs) == 1:
        outs[0][...] = sp_ref[...] + late_ref[...]
        return
    half = L // 2
    low = lax.axis_index("trc") == 0
    for keeps_low in (True, False):

        @pl.when(low if keeps_low else jnp.logical_not(low))
        def _(keeps_low=keeps_low):
            for out, first in zip(outs, (keeps_low, not keeps_low)):
                k0 = 0 if first else half
                out[...] = sp_ref[:, k0 : k0 + half] + late_ref[:, k0 : k0 + half]


def start_edge_body(dims, *refs):
    T, L, C, _ = dims
    qe, fe, de, le = refs[:4]
    kept = refs[4:8]
    out_hbm, out_ref, acc, sem = refs[9:]

    def done(k, c, value):
        out_ref[pl.ds(k * C + c, T, stride=L * C), :] = value

    fields = Fields(fe, de, lax.axis_index("lev") * L)
    adjoint(dims, fields, qe, H, le, acc, done, parts(C)[0], kept=kept)
    copy = pltpu.make_async_copy(out_ref, out_hbm, sem)
    copy.start()
    copy.wait()


def f32(*shape):
    return jax.ShapeDtypeStruct(shape, jnp.float32)


def call(body, outs, scratch, args, hbm=0, aliases=None, mib=4, hbm_out=0):
    return run(body, outs, scratch, args, hbm, aliases, mib, hbm_out)


def run(body, outs, scratch, args, hbm, aliases, mib, hbm_out):
    vmem = pl.BlockSpec(memory_space=pltpu.VMEM)
    return pl.pallas_call(
        body,
        out_shape=outs,
        in_specs=[pl.BlockSpec(memory_space=pltpu.HBM)] * hbm + [vmem] * (len(args) - hbm),
        out_specs=[pl.BlockSpec(memory_space=pltpu.HBM)] * hbm_out + [vmem] * (len(outs) - hbm_out),
        scratch_shapes=scratch,
        input_output_aliases=aliases or {},
        compiler_params=pltpu.CompilerParams(vmem_limit_bytes=mib * 1024 * 1024),
    )(*args)


def swap(values, axis, pairings_):
    received = []
    for x, pairs in zip(values, pairings_):
        received.append(lax.ppermute(x, axis, pairs))
    return received


def program(tracers, cotangent, zonal_speed, meridional_speed, vertical_speed, lateral_mixing, vertical_mixing, column_depth):
    dims = T, L, C, Y = tracers.shape
    tile_pairs = pairings(lax.axis_size("tile"))
    lev_pairs = pairings(lax.axis_size("lev"))
    n_tile, n_lev = len(tile_pairs), len(lev_pairs)
    q = tracers.reshape(T * L * C, Y)
    l = cotangent.reshape(T * L * C, Y)
    inputs = [q, l, zonal_speed, meridional_speed, vertical_speed, lateral_mixing, vertical_mixing, column_depth]
    inputs = [pltpu.with_memory_space_constraint(x, pltpu.HBM) for x in inputs]
    tile_rows = H * T + FPAD
    lev_rows = max(C * T, W * NF * C)
    *to_tile, q, l, f, d = call(
        functools.partial(edges_body, dims, n_tile),
        [f32(L, tile_rows, Y)] * n_tile
        + [f32(T * L * C, Y)] * 2
        + [f32(NF, L, C, Y), jax.ShapeDtypeStruct((C, Y), jnp.int32)],
        [pltpu.SemaphoreType.DMA((8,))],
        inputs,
        hbm=8,
        mib=MIB,
    )
    from_tile = swap(to_tile, "tile", tile_pairs)

    qe_s = f32(L + 2 * H, C + 2 * H, T, Y)
    ext_s = f32(L + 2 * E, C + 2 * E, T, Y)
    fe_s = f32(NF, L + 2 * W, C + 2 * W, 1, Y)
    de_s = f32(3, C + 2 * W, 1, Y)
    own_s = f32(L, C, T, Y)
    sent = call(
        functools.partial(own_body, dims, n_tile, n_lev),
        [f32(L, E, T, Y)] * n_tile + [f32(H + E + 1, lev_rows, Y)] * n_lev + [qe_s, ext_s, fe_s, de_s],
        [],
        [q, l, f, d],
    )
    qe, le, fe, de = sent[n_tile + n_lev :]
    from_lev = swap(sent[n_tile : n_tile + n_lev], "lev", lev_pairs)
    late_tile = swap(sent[:n_tile], "tile", tile_pairs)
    me, yu, yd, yc = call(functools.partial(inner_y_body, dims), [ext_s] + [own_s] * 3, [], [qe, fe, de])
    n = n_lev
    qe, le, fe, me, vu, vd, vc = call(
        functools.partial(inner_v_body, dims, n_lev),
        [qe_s, ext_s, fe_s, ext_s] + [f32(L + 2, C, T, Y)] * 2 + [own_s],
        [],
        [*from_lev, qe, le, fe, me, de],
        aliases={n + i: i for i in range(4)},
    )
    to_lev = call(
        functools.partial(corner_body, dims, n_tile), [f32(n_tile, E, tile_rows, Y)] * n_lev, [], [*from_tile, me]
    )
    corners = swap(to_lev, "lev", lev_pairs)
    n = n_tile
    qe, fe, de, me, zc = call(
        functools.partial(beside_body, dims, n_tile),
        [qe_s, fe_s, de_s, ext_s, own_s],
        [],
        [*from_tile, qe, fe, de, me],
        aliases={n + i: i for i in range(4)},
    )
    n = n_lev + n_tile
    qe, le, fe, me, mc, late, *mc_edges = call(
        functools.partial(late_body, dims, n_tile, n_lev),
        [qe_s, ext_s, fe_s, ext_s, own_s, f32(3, L, C, Y)] + [f32(L, E, T, Y)] * n_tile,
        [],
        [*corners, *late_tile, de, qe, le, fe, me],
        aliases={n + 1 + i: i for i in range(4)},
    )
    mc_tile = swap(mc_edges, "tile", tile_pairs)
    mc, late, *mc_edges = call(
        functools.partial(late_inner_body, dims),
        [own_s, f32(3, L, C, Y)] + [f32(E, C, T, Y)] * n_lev,
        [],
        [le, fe, de, me, mc, late],
        aliases={4: 0, 5: 1},
    )
    mc_lev = swap(mc_edges, "lev", lev_pairs)
    le, acc = call(functools.partial(start_inner_body, dims), [ext_s, own_s], [], [qe, fe, de, mc, yu, yd])
    le, out = call(
        functools.partial(start_levels_body, dims, n_lev),
        [ext_s, f32(T * L * C, Y)],
        [],
        [fe, de, vu, vd, acc, *mc_lev, le],
        aliases={5 + n_lev: 0},
    )
    pair = lax.axis_size("trc") == 2 and L % 2 == 0
    le, speeds, *given = call(
        functools.partial(speeds_body, dims, n_tile),
        [ext_s] + ([f32(3, L // 2, C, Y)] * 2 if pair else [f32(3, L, C, Y)]),
        [pltpu.VMEM((3, L, C, Y), jnp.float32)],
        [fe, de, late, zc, yc, vc, *mc_tile, le],
        aliases={6 + n_tile: 0},
    )
    if pair:
        other = swap(given, "trc", [[(0, 1), (1, 0)]])[0]
    start, _ = call(
        functools.partial(start_edge_body, dims),
        [f32(T * L * C, Y)] * 2,
        [pltpu.VMEM(own_s.shape, jnp.float32), pltpu.SemaphoreType.DMA],
        [qe, fe, de, le, yu, yd, vu, vd, out],
        aliases={8: 1},
        hbm_out=1,
    )
    speeds = speeds + other if pair else lax.psum_scatter(speeds, "trc", scatter_dimension=1, tiled=True)
    return start.reshape(T, L, C, Y), speeds


def solution(mesh):
    return jax.shard_map(
        program,
        mesh=mesh,
        in_specs=(
            P("trc", "lev", ("ens", "tile"), None),
            P("trc", "lev", ("ens", "tile"), None),
            P("lev", ("ens", "tile"), None),
            P("lev", ("ens", "tile"), None),
            P("lev", ("ens", "tile"), None),
            P("lev", ("ens", "tile"), None),
            P("lev", ("ens", "tile"), None),
            P(("ens", "tile"), None),
        ),
        out_specs=(
            P("trc", "lev", ("ens", "tile"), None),
            P(None, ("lev", "trc"), ("ens", "tile"), None),
        ),
        check_vma=False,
    )
```

```python
import functools

import jax
import jax.numpy as jnp
from jax import lax
from jax.experimental import pallas as pl
from jax.experimental.pallas import tpu as pltpu
from jax.sharding import PartitionSpec as P

albada_floor = 0.01
H = 4
E = 2
W = 3
NF = 5
MIB = 4
FPAD = 16


def pairings(count):
    phases = []
    for first in (0, 1):
        pairs = []
        for i in range(first, count - 1, 2):
            pairs += [(i, i + 1), (i + 1, i)]
        if pairs:
            phases.append(pairs)
    return phases


def by_parity(even, phase, act):
    @pl.when(even)
    def _():
        act(phase == 0)

    @pl.when(jnp.logical_not(even))
    def _():
        act(phase == 1)


def limiter(x, y, xx, yy):
    s = x * y
    r = 1.0 / (xx + yy + albada_floor)
    a = s * (x + y) * r
    return s, r, a


def slopes(x, y, xx, yy, s, r, a):
    return r * (0.5 * yy + s - x * a), r * (0.5 * xx + s - y * a)


def forward_chain(n, get_u, get_co, emit, keep=None):
    u_a, u_b = get_u(-2), get_u(-1)
    d_b = u_b - u_a
    xx_b = d_b * d_b
    half_b = None
    flux_b = None
    for f in range(0, n + 2):
        u_c = get_u(f)
        d_c = u_c - u_b
        xx_c = d_c * d_c
        s, r, a = limiter(d_b, d_c, xx_b, xx_c)
        half_c = 0.5 * a
        carried = None
        if f >= 1:
            v, m = get_co(f - 1)
            carried = jnp.where(v >= 0.0, u_a + half_b, u_b - half_c)
            flux = v * carried - m * d_b
            if f >= 2:
                emit(f - 2, flux_b - flux)
            flux_b = flux
        if keep is not None:
            keep(f - 1, lambda: slopes(d_b, d_c, xx_b, xx_c, s, r, a), carried)
        u_a, u_b, d_b, xx_b, half_b = u_b, u_c, d_c, xx_c, half_c


def fresh_limits(get_u):
    state = {"u_a": get_u(-2), "u_b": get_u(-1), "half": None}
    state["d"] = state["u_b"] - state["u_a"]
    state["xx"] = state["d"] * state["d"]

    def step(f, v):
        u_a, u_b, d_b, xx_b = state["u_a"], state["u_b"], state["d"], state["xx"]
        u_c = get_u(f)
        d_c = u_c - u_b
        xx_c = d_c * d_c
        s, r, a = limiter(d_b, d_c, xx_b, xx_c)
        half_c = 0.5 * a
        carried = None
        if f >= 1:
            carried = jnp.where(v >= 0.0, u_a + state["half"], u_b - half_c)
        state.update(u_a=u_b, u_b=u_c, half=half_c, d=d_c, xx=xx_c)
        up, down = slopes(d_b, d_c, xx_b, xx_c, s, r, a)
        return up, down, carried

    return step


def adjoint_chain(n, limits, get_l, get_co, emit, emit_speed):
    l_b = get_l(-1)
    g_b = l_b - get_l(-2)
    v_b, _ = get_co(-1)
    n_b = jnp.minimum(v_b, 0.0) * g_b
    p_b = dm_b = down_a = dd_a = n_a = None
    for f in range(0, n + 2):
        l_c = get_l(f)
        g_c = l_c - l_b
        v_c, m_c = get_co(f)
        p_c = jnp.maximum(v_c, 0.0) * g_c
        n_c = jnp.minimum(v_c, 0.0) * g_c
        up, down, carried = limits(f, v_b)
        e = p_c - n_b
        if f >= 1:
            dd_b = e * up + down_a - dm_b
            if f >= 2:
                emit(f - 2, n_a + p_b + dd_a - dd_b)
            if emit_speed is not None and f - 1 < n:
                emit_speed(f - 1, g_b * carried)
            dd_a = dd_b
        down_a = e * down
        n_a = n_b
        p_b, n_b, v_b = p_c, n_c, v_c
        dm_b = m_c * g_c
        g_b, l_b = g_c, l_c


def lanes(T, Y):
    lane = lax.broadcasted_iota(jnp.int32, (T, Y), 1)
    return lane == 0, lane == Y - 1


def along_values(u, v, ends):
    first, last = ends
    Y = u.shape[-1]
    before = jnp.where(first, 0.0, pltpu.roll(u, 1, 1))
    d = u - before
    nxt = jnp.where(last, 0.0, pltpu.roll(u, Y - 1, 1)) - u
    xx, yy = d * d, nxt * nxt
    s, r, a = limiter(d, nxt, xx, yy)
    half = 0.5 * a
    carried = jnp.where(v >= 0.0, before + pltpu.roll(half, 1, 1), u - half)
    return d, carried, lambda: slopes(d, nxt, xx, yy, s, r, a)


def along_forward(d, carried, v, m):
    flux = v * carried - m * d
    return flux - pltpu.roll(flux, flux.shape[-1] - 1, 1)


def along_adjoint(l, v, m, up, down, ends):
    first, last = ends
    Y = l.shape[-1]
    g = l - pltpu.roll(l, 1, 1)
    n = jnp.minimum(v, 0.0) * g
    p_next = pltpu.roll(jnp.maximum(v, 0.0), Y - 1, 1) * (pltpu.roll(l, Y - 1, 1) - l)
    e = p_next - n
    z = e * up - m * g
    y = e * down
    add = (
        (n + z - y + p_next)
        + jnp.where(first, 0.0, pltpu.roll(y, 1, 1))
        - jnp.where(last, 0.0, pltpu.roll(z, Y - 1, 1))
    )
    return add, g


class Fields:
    def __init__(self, f_ref, d_ref, level0):
        self.f, self.d, self.level0 = f_ref, d_ref, level0

    def open(self, direction, k, c):
        level = (self.level0 + k).astype(jnp.float32)
        if direction == 2:
            level = jnp.where(level >= 1.0, level, 1e9)
        return self.d[direction, W + c] > level

    def at(self, direction, k, c):
        is_open = self.open(direction, k, c)
        speed = self.f[direction, W + k, W + c]
        mix = self.f[(3, 3, 4)[direction], W + k, W + c]
        return jnp.where(is_open, speed, 0.0), jnp.where(is_open, mix, 0.0), is_open


def parities():
    return lax.axis_index("tile") % 2 == 0, lax.axis_index("lev") % 2 == 0


def depth_rows(de, columns):
    Y = de.shape[-1]
    lane0 = lax.broadcasted_iota(jnp.int32, (1, Y), 1) == 0
    for c in columns:
        here = de[2, W + c]
        de[1, W + c] = jnp.where(lane0, 0.0, jnp.minimum(pltpu.roll(here, 1, 1), here))


def edges_body(dims, n_tile, *refs):
    T, L, C, _ = dims
    sources, tile_out, (q_ref, l_ref, f_ref, d_ref, sem) = refs[:8], refs[8 : 8 + n_tile], refs[8 + n_tile :]
    targets = [q_ref, l_ref] + [f_ref.at[f] for f in range(NF)] + [d_ref]
    order = [0] + list(range(2, 8)) + [1]
    copies = [pltpu.make_async_copy(sources[i], targets[i], sem.at[i]) for i in order]
    for c in copies:
        c.start()
    for c in copies[1:-1] + copies[:1]:
        c.wait()
    tile_even, _ = parities()

    for phase, out in enumerate(tile_out):

        def send_tile(high, out=out):
            q0 = C - H if high else 0
            f0 = C - W if high else 0

            def level(k, carry):
                for j in range(H):
                    out[k, j * T : (j + 1) * T, :] = q_ref[pl.ds(k * C + q0 + j, T, stride=L * C), :]
                for f in range(NF):
                    r = H * T + W * f
                    out[k, r : r + W, :] = f_ref[f, k, f0 : f0 + W, :]
                r = H * T + W * NF
                out[k, r : r + 1, :] = d_ref[f0 : f0 + 1, :].astype(jnp.float32)
                return carry

            lax.fori_loop(0, L, level, 0, unroll=2)
            r = H * T + W * NF
            for j in range(1, W):
                out[j, r : r + 1, :] = d_ref[f0 + j : f0 + j + 1, :].astype(jnp.float32)

        by_parity(tile_even, phase, send_tile)
    copies[-1].wait()


def own_body(dims, n_tile, n_lev, *refs):
    T, L, C, Y = dims
    q_ref, l_ref, f_ref, d_ref = refs[:4]
    tile_out, lev_out = refs[4 : 4 + n_tile], refs[4 + n_tile : 4 + n_tile + n_lev]
    qe, le, fe, de = refs[4 + n_tile + n_lev :]
    tile_even, lev_even = parities()
    zero = jnp.zeros((T, Y), jnp.float32)
    zero_row = jnp.zeros((1, Y), jnp.float32)

    def own_level(k, carry):
        for c in range(C):
            qe[H + k, H + c] = q_ref[pl.ds(k * C + c, T, stride=L * C), :]
            le[E + k, E + c] = l_ref[pl.ds(k * C + c, T, stride=L * C), :]
            for f in range(NF):
                fe[f, W + k, W + c] = f_ref[f, k, c : c + 1, :]
        return carry

    lax.fori_loop(0, L, own_level, 0)
    for c in range(C):
        de[2, W + c] = d_ref[c : c + 1, :].astype(jnp.float32)
    depth_rows(de, range(C))

    for phase, out in enumerate(tile_out):

        def send_tile(high, out=out):
            def level(k, carry):
                for j in range(E):
                    out[k, j] = le[E + k, E + (C - E if high else 0) + j]
                return carry

            lax.fori_loop(0, L, level, 0, unroll=2)

        by_parity(tile_even, phase, send_tile)

    for phase, out in enumerate(lev_out):

        def send_lev(high, out=out):
            def column(c, carry):
                rows = pl.ds(pl.multiple_of(c * T, 8), T)
                for j in range(H):
                    out[j, rows, :] = qe[H + (L - H if high else 0) + j, H + c]
                for j in range(E):
                    out[H + j, rows, :] = le[E + (L - E if high else 0) + j, E + c]
                return carry

            lax.fori_loop(0, C, column, 0)
            for j in range(W):
                k = (L - W if high else 0) + j
                for f in range(NF):
                    out[H + E, (j * NF + f) * C : (j * NF + f + 1) * C, :] = f_ref[f, k]

        by_parity(lev_even, phase, send_lev)

    def blank_lev(high):
        def column(c, carry):
            for j in range(H):
                qe[(H + L if high else 0) + j, H + c] = zero
            for j in range(E):
                le[(E + L if high else 0) + j, E + c] = zero
            for j in range(W):
                for f in range(NF):
                    fe[f, (W + L if high else 0) + j, W + c] = zero_row
            return carry

        lax.fori_loop(0, C, column, 0)
        for j in range(E):
            for i in range(E):
                for col in (H - E + i, H + C + i):
                    qe[(H + L if high else H - E) + j, col] = zero
                for f in range(NF):
                    for col in (W - E + i, W + C + i):
                        fe[f, (W + L if high else W - E) + j, col] = zero_row

    for phase in range(n_lev, 2):
        by_parity(lev_even, phase, blank_lev)


def inner_y_body(dims, qe, fe, de, me, ky):
    T, L, C, Y = dims
    fields = Fields(fe, de, lax.axis_index("lev") * L)
    ends = lanes(T, Y)

    def own_y(k, carry):
        for c in range(C):
            u = qe[H + k, H + c]
            v, m, _ = fields.at(1, k, c)
            d, carried, coefs = along_values(u, v, ends)
            ky[k, c, 0], ky[k, c, 1] = coefs()
            ky[k, c, 2] = carried
            me[E + k, E + c] = u + along_forward(d, carried, v, m)
        return carry

    lax.fori_loop(0, L, own_y, 0)


def inner_v_body(dims, n_lev, *refs):
    T, L, C, Y = dims
    lev_in = refs[:n_lev]
    de = refs[n_lev + 4]
    qe, le, fe, me, kv = refs[n_lev + 5 :]
    _, lev_even = parities()
    zero = jnp.zeros((T, Y), jnp.float32)

    for phase, source in enumerate(lev_in):

        def place_lev(high, source=source):
            q0 = H + L if high else 0
            l0 = E + L if high else 0
            f0 = W + L if high else 0

            def column(c, carry):
                rows = pl.ds(pl.multiple_of(c * T, 8), T)
                for j in range(H):
                    qe[q0 + j, H + c] = source[j, rows, :]
                for j in range(E):
                    le[l0 + j, E + c] = source[H + j, rows, :]
                return carry

            lax.fori_loop(0, C, column, 0)
            for j in range(W):
                for f in range(NF):
                    for c in range(C):
                        r = (j * NF + f) * C + c
                        fe[f, f0 + j, W + c] = source[H + E, r : r + 1, :]

        by_parity(lev_even, phase, place_lev)

    fields = Fields(fe, de, lax.axis_index("lev") * L)
    ends = lanes(T, Y)

    for phase in range(2):
        if phase < n_lev:
            high = lev_even if phase == 0 else jnp.logical_not(lev_even)
            k0 = jnp.where(high, L, -E)

            def beside(i, carry, k0=k0):
                k = k0 + i
                for c in range(C):
                    u = qe[H + k, H + c]
                    v, m, _ = fields.at(1, k, c)
                    d, carried, _ = along_values(u, v, ends)
                    me[E + k, E + c] = u + along_forward(d, carried, v, m)
                return carry

            lax.fori_loop(0, E, beside, 0)
        else:

            def blank(high):
                def column(c, carry):
                    for j in range(E):
                        me[(E + L if high else 0) + j, E + c] = zero
                    return carry

                lax.fori_loop(0, C, column, 0)

            by_parity(lev_even, phase, blank)

    def own_v(c, carry):
        def emit(k, value):
            me[k, E + c] = me[k, E + c] + value

        def keep(k, coefs, carried):
            k = k - E
            if -1 <= k <= L:
                kv[1 + k, c, 0], kv[1 + k, c, 1] = coefs()
            if 0 <= k < L:
                kv[1 + k, c, 2] = carried

        forward_chain(
            L + 2 * E, lambda k: qe[H - E + k, H + c], lambda k: fields.at(2, k - E, c)[:2], emit, keep
        )
        return carry

    lax.fori_loop(0, C, own_v, 0)


def corner_body(dims, n_tile, *refs):
    L = dims[1]
    tile_in, lev_out = refs[:n_tile], refs[n_tile + 1 :]
    _, lev_even = parities()
    for phase, out in enumerate(lev_out):

        def send(high, out=out):
            for t in range(n_tile):
                for j in range(E):
                    out[t, j] = tile_in[t][(L - E if high else 0) + j]

        by_parity(lev_even, phase, send)


def beside_body(dims, n_tile, *refs):
    T, L, C, Y = dims
    tile_in = refs[:n_tile]
    qe, fe, de, me, zc = refs[n_tile + 4 :]
    tile_even, _ = parities()
    zero = jnp.zeros((T, Y), jnp.float32)
    zero_row = jnp.zeros((1, Y), jnp.float32)

    def place_tile(source, high):
        q0 = H + C if high else 0
        f0 = W + C if high else 0

        def level(k, carry):
            for j in range(H):
                qe[H + k, q0 + j] = zero if source is None else source[k, j * T : (j + 1) * T, :]
            base = H * T
            for f in range(NF):
                for j in range(W):
                    r = base + W * f + j
                    fe[f, W + k, f0 + j] = zero_row if source is None else source[k, r : r + 1, :]
            return carry

        lax.fori_loop(0, L, level, 0, unroll=4)
        base = H * T + W * NF
        for j in range(W):
            de[2, f0 + j] = zero_row if source is None else source[j, base : base + 1, :]

    for phase in range(2):
        source = tile_in[phase] if phase < n_tile else None
        by_parity(tile_even, phase, lambda high, s=source: place_tile(s, high))

    depth_rows(de, [-2, -1, C, C + 1])
    for c in range(-E, C + E + 1):
        de[0, W + c] = jnp.minimum(de[2, W + c - 1], de[2, W + c])

    fields = Fields(fe, de, lax.axis_index("lev") * L)
    ends = lanes(T, Y)

    def level_y(k, carry):
        for c in (-2, -1, C, C + 1):
            u = qe[H + k, H + c]
            v, m, _ = fields.at(1, k, c)
            d, carried, _ = along_values(u, v, ends)
            me[E + k, E + c] = u + along_forward(d, carried, v, m)
        return carry

    lax.fori_loop(0, L, level_y, 0, unroll=2)

    def level_z(k, carry):
        def emit(c, value):
            me[E + k, c] = me[E + k, c] + value

        def keep(c, coefs, carried):
            if 0 <= c - E < C:
                zc[k, c - E] = carried

        forward_chain(
            C + 2 * E, lambda c: qe[H + k, H - E + c], lambda c: fields.at(0, k, c - E)[:2], emit, keep
        )
        return carry

    lax.fori_loop(0, L, level_z, 0)


def late_body(dims, n_tile, n_lev, *refs):
    T, L, C, Y = dims
    corner_in, tile_in = refs[:n_lev], refs[n_lev : n_lev + n_tile]
    de = refs[n_lev + n_tile]
    qe, le, fe, me, mc_ref, sp_ref, *tile_out = refs[n_lev + n_tile + 5 :]
    tile_even, lev_even = parities()
    zero = jnp.zeros((T, Y), jnp.float32)
    zero_row = jnp.zeros((1, Y), jnp.float32)

    def place_corner(source, tile_high, lev_high):
        for j in range(E):
            q_lev = H + L + j if lev_high else H - E + j
            f_lev = W + L + j if lev_high else W - E + j
            for i in range(E):
                s = i if tile_high else H - E + i
                col = (H + C + i) if tile_high else (H - E + i)
                qe[q_lev, col] = zero if source is None else source[j, s * T : (s + 1) * T, :]
                for f in range(NF):
                    r = H * T + W * f + (i if tile_high else W - E + i)
                    col = (W + C + i) if tile_high else (W - E + i)
                    fe[f, f_lev, col] = zero_row if source is None else source[j, r : r + 1, :]

    for phase in range(n_lev):
        for other in range(2):

            def corner(lev_high, p=phase, t=other):
                source = corner_in[p].at[t] if t < n_tile else None
                by_parity(tile_even, t, lambda tile_high: place_corner(source, tile_high, lev_high))

            by_parity(lev_even, phase, corner)

    def place_tile(source, high):
        def level(k, carry):
            for j in range(E):
                le[E + k, (E + C if high else 0) + j] = zero if source is None else source[k, j]
            return carry

        lax.fori_loop(0, L, level, 0, unroll=2)

    for phase in range(2):
        source = tile_in[phase] if phase < n_tile else None
        by_parity(tile_even, phase, lambda high, s=source: place_tile(s, high))

    fields = Fields(fe, de, lax.axis_index("lev") * L)

    for phase in range(n_lev):
        high = lev_even if phase == 0 else jnp.logical_not(lev_even)
        k0 = jnp.where(high, L, -E)

        def beside(j, carry, k0=k0):
            k = k0 + j

            def emit(c, value):
                me[E + k, E + c] = me[E + k, E + c] + value

            forward_chain(C, lambda c: qe[H + k, H + c], lambda c: fields.at(0, k, c)[:2], emit)
            return carry

        lax.fori_loop(0, E, beside, 0)

    def side_v(i, carry):
        c = jnp.where(i < E, i - E, C - E + i)

        def emit(k, value):
            me[E + k, E + c] = me[E + k, E + c] + value

        forward_chain(L, lambda k: qe[H + k, H + c], lambda k: fields.at(2, k, c)[:2], emit)
        return carry

    lax.fori_loop(0, 2 * E, side_v, 0)

    def done(k, c, value):
        mc_ref[k, c] = value

    adjoint(dims, fields, me, E, le, mc_ref, done, parts(C)[0], sp_ref)

    for phase, out in enumerate(tile_out):

        def send_tile(high, out=out):
            def level(k, carry):
                for j in range(E):
                    out[k, j] = mc_ref[k, (C - E if high else 0) + j]
                return carry

            lax.fori_loop(0, L, level, 0, unroll=2)

        by_parity(tile_even, phase, send_tile)


def late_inner_body(dims, *refs):
    _, L, C, _ = dims
    le, fe, de, me = refs[:4]
    mc_ref, sp_ref, *lev_out = refs[6:]
    _, lev_even = parities()

    def done(k, c, value):
        mc_ref[k, c] = value

    fields = Fields(fe, de, lax.axis_index("lev") * L)
    adjoint(dims, fields, me, E, le, mc_ref, done, parts(C)[1], sp_ref)

    for phase, out in enumerate(lev_out):

        def send_lev(high, out=out):
            def column(c, carry):
                for j in range(E):
                    out[j, c] = mc_ref[(L - E if high else 0) + j, c]
                return carry

            lax.fori_loop(0, C, column, 0, unroll=2)

        by_parity(lev_even, phase, send_lev)


def parts(C):
    edge = (list(range(E)) + list(range(C - E, C)), [(0, E), (C - E, E)], lambda i: jnp.where(i < E, i, C - 2 * E + i))
    inner = (list(range(E, C - E)), [(E, C - 2 * E)] if C > 2 * E else [], lambda i: E + i)
    both = (list(range(C)), [(0, C)], lambda i: i)
    return edge, inner, both


def adjoint(dims, fields, u_ref, uo, l_ref, acc_ref, done, part, speed_ref=None, kept=None, passes="yzv", level_done=None):
    T, L, _, Y = dims
    ends = lanes(T, Y)
    ky, kv = kept or (None, None)
    columns, runs, column_of = part

    def put(direction, k, c, value):
        value = acc_ref[k, c] + value
        if done is not None and direction == passes[-1]:
            done(k, c, value)
        else:
            acc_ref[k, c] = value

    def store_speed(direction, k, c, is_open, value):
        if speed_ref is not None:
            row = jnp.sum(value, axis=0, keepdims=True)
            speed_ref[direction, k, pl.ds(c, 1), :] = jnp.where(is_open, row, 0.0)

    def along(k, carry):
        for c in columns:
            l = l_ref[E + k, E + c]
            v, m, is_open = fields.at(1, k, c)
            if kept is None:
                _, carried, coefs = along_values(u_ref[uo + k, uo + c], v, ends)
                up, down = coefs()
            else:
                up, down = ky[k, c, 0], ky[k, c, 1]
            add, g = along_adjoint(l, v, m, up, down, ends)
            acc_ref[k, c] = l + add
            if speed_ref is not None:
                store_speed(1, k, c, is_open, g * carried)
        return carry

    def level_z(k, carry):
        for c0, n in runs:
            opened = {}

            def co(c, c0=c0, opened=opened):
                v, m, opened[c] = fields.at(0, k, c0 + c)
                return v, m

            def emit(c, value, c0=c0):
                put("z", k, c0 + c, value)

            def speed(c, value, c0=c0, opened=opened):
                store_speed(0, k, c0 + c, opened[c], value)

            adjoint_chain(
                n,
                fresh_limits(lambda c, c0=c0: u_ref[uo + k, uo + c0 + c]),
                lambda c, c0=c0: l_ref[E + k, E + c0 + c],
                co,
                emit,
                speed if speed_ref is not None else None,
            )
        if level_done is not None:
            level_done(k)
        return carry

    def column_v(i, carry):
        c = column_of(i)
        opened = {}

        def co(k):
            v, m, opened[k] = fields.at(2, k, c)
            return v, m

        def emit(k, value):
            put("v", k, c, value)

        if kept is None or kv is None:
            limits = fresh_limits(lambda k: u_ref[uo + k, uo + c])
        else:

            def limits(f, v):
                return kv[f, c, 0], kv[f, c, 1], None

        adjoint_chain(
            L,
            limits,
            lambda k: l_ref[E + k, E + c],
            co,
            emit,
            (lambda k, value: store_speed(2, k, c, opened[k], value)) if speed_ref is not None else None,
        )
        return carry

    for direction in passes:
        if direction == "y":
            lax.fori_loop(0, L, along, 0, unroll=2 if len(columns) <= 4 else 1)
        elif direction == "z":
            lax.fori_loop(0, L, level_z, 0)
        else:
            lax.fori_loop(0, len(columns), column_v, 0)


def start_inner_body(dims, *refs):
    _, L, C, _ = dims
    qe, fe, de, mc_ref, ky, le, acc = refs

    def own(k, carry):
        for c in range(C):
            le[E + k, E + c] = mc_ref[k, c]
        return carry

    lax.fori_loop(0, L, own, 0, unroll=2)
    fields = Fields(fe, de, lax.axis_index("lev") * L)
    adjoint(dims, fields, qe, H, le, acc, None, parts(C)[1], kept=(ky, None), passes="yz")


def start_levels_body(dims, n_lev, *refs):
    T, L, C, Y = dims
    fe, de, kv, ky, zc, late_ref = refs[:6]
    lev_in = refs[6 : 6 + n_lev]
    le, sp_ref = refs[7 + n_lev :]
    _, lev_even = parities()
    zero = jnp.zeros((T, Y), jnp.float32)

    def place_lev(source, high):
        def column(c, carry):
            for j in range(E):
                le[(E + L if high else 0) + j, E + c] = zero if source is None else source[j, c]
            return carry

        lax.fori_loop(0, C, column, 0, unroll=2)

    for phase in range(2):
        source = lev_in[phase] if phase < n_lev else None
        by_parity(lev_even, phase, lambda high, s=source: place_lev(s, high))

    fields = Fields(fe, de, lax.axis_index("lev") * L)

    def level(k, carry):
        for c in range(C):
            l = le[E + k, E + c]
            befores = (le[E + k, E + c - 1] if c > 0 else None, pltpu.roll(l, 1, 1), le[E + k - 1, E + c])
            values = (zc[k, c], ky[k, c, 2], kv[k + 1, c, 2])
            for direction, before, carried in zip(range(3), befores, values):
                row = late_ref[direction, k, c : c + 1, :]
                if before is not None:
                    row = row + face_row(fields, direction, k, c, l - before, carried)
                sp_ref[direction, k, c : c + 1, :] = row
        return carry

    lax.fori_loop(0, L, level, 0)


def face_row(fields, direction, k, c, difference, carried):
    row = jnp.sum(difference * carried, axis=0, keepdims=True)
    return jnp.where(fields.open(direction, k, c), row, 0.0)


def speeds_body(dims, n_tile, *refs):
    T, L, C, Y = dims
    fe, de, part_ref, zc = refs[:4]
    tile_in = refs[4 : 4 + n_tile]
    le, *outs, row_ref = refs[5 + n_tile :]
    tile_even, _ = parities()
    zero = jnp.zeros((T, Y), jnp.float32)

    def place_tile(source, high):
        def level(k, carry):
            for j in range(E):
                le[E + k, (E + C if high else 0) + j] = zero if source is None else source[k, j]
            return carry

        lax.fori_loop(0, L, level, 0, unroll=2)

    for phase in range(2):
        source = tile_in[phase] if phase < n_tile else None
        by_parity(tile_even, phase, lambda high, s=source: place_tile(s, high))

    fields = Fields(fe, de, lax.axis_index("lev") * L)

    for k in range(L):
        row_ref[k : k + 1, :] = face_row(fields, 0, k, 0, le[E + k, E] - le[E + k, E - 1], zc[k, 0])

    def put(out, k0, n):
        out[...] = part_ref[:, k0 : k0 + n]
        for k in range(n):
            out[0, k, 0:1, :] = out[0, k, 0:1, :] + row_ref[k0 + k : k0 + k + 1, :]

    if len(outs) == 1:
        put(outs[0], 0, L)
        return
    half = L // 2
    low = lax.axis_index("trc") == 0
    for keeps_low in (True, False):

        @pl.when(low if keeps_low else jnp.logical_not(low))
        def _(keeps_low=keeps_low):
            for out, first in zip(outs, (keeps_low, not keeps_low)):
                put(out, 0 if first else half, half)


def start_edge_body(dims, *refs):
    T, L, C, Y = dims
    qe, fe, de, le, ky, kv = refs[:6]
    out_hbm, acc, out_ref, sem = refs[7:]
    flat = out_ref.reshape(T * L * C, Y)

    def done(k, c, value):
        flat[pl.ds(k * C + c, T, stride=L * C), :] = value

    def leaving(k):
        return pltpu.make_async_copy(out_ref.at[:, k], out_hbm.at[:, k], sem.at[k])

    fields = Fields(fe, de, lax.axis_index("lev") * L)
    kept = (ky, kv)
    edge, inner = parts(C)[:2]
    adjoint(dims, fields, qe, H, le, acc, None, edge, kept=kept, passes="y")
    adjoint(dims, fields, qe, H, le, acc, done, inner, kept=kept, passes="v")
    adjoint(
        dims, fields, qe, H, le, acc, done, edge, kept=kept, passes="vz", level_done=lambda k: leaving(k).start()
    )
    for k in range(L):
        leaving(k).wait()


def f32(*shape):
    return jax.ShapeDtypeStruct(shape, jnp.float32)


def call(body, outs, scratch, args, hbm=0, aliases=None, mib=4, hbm_out=0):
    return run(body, outs, scratch, args, hbm, aliases, mib, hbm_out)


def run(body, outs, scratch, args, hbm, aliases, mib, hbm_out):
    vmem = pl.BlockSpec(memory_space=pltpu.VMEM)
    return pl.pallas_call(
        body,
        out_shape=outs,
        in_specs=[pl.BlockSpec(memory_space=pltpu.HBM)] * hbm + [vmem] * (len(args) - hbm),
        out_specs=[pl.BlockSpec(memory_space=pltpu.HBM)] * hbm_out + [vmem] * (len(outs) - hbm_out),
        scratch_shapes=scratch,
        input_output_aliases=aliases or {},
        compiler_params=pltpu.CompilerParams(vmem_limit_bytes=mib * 1024 * 1024),
    )(*args)


def swap(values, axis, pairings_):
    received = []
    for x, pairs in zip(values, pairings_):
        received.append(lax.ppermute(x, axis, pairs))
    return received


def program(tracers, cotangent, zonal_speed, meridional_speed, vertical_speed, lateral_mixing, vertical_mixing, column_depth):
    dims = T, L, C, Y = tracers.shape
    tile_pairs = pairings(lax.axis_size("tile"))
    lev_pairs = pairings(lax.axis_size("lev"))
    n_tile, n_lev = len(tile_pairs), len(lev_pairs)
    q = tracers.reshape(T * L * C, Y)
    l = cotangent.reshape(T * L * C, Y)
    inputs = [q, l, zonal_speed, meridional_speed, vertical_speed, lateral_mixing, vertical_mixing, column_depth]
    inputs = [pltpu.with_memory_space_constraint(x, pltpu.HBM) for x in inputs]
    tile_rows = H * T + FPAD
    lev_rows = max(C * T, W * NF * C)
    *to_tile, q, l, f, d = call(
        functools.partial(edges_body, dims, n_tile),
        [f32(L, tile_rows, Y)] * n_tile
        + [f32(T * L * C, Y)] * 2
        + [f32(NF, L, C, Y), jax.ShapeDtypeStruct((C, Y), jnp.int32)],
        [pltpu.SemaphoreType.DMA((8,))],
        inputs,
        hbm=8,
        mib=MIB,
    )
    from_tile = swap(to_tile, "tile", tile_pairs)

    qe_s = f32(L + 2 * H, C + 2 * H, T, Y)
    ext_s = f32(L + 2 * E, C + 2 * E, T, Y)
    fe_s = f32(NF, L + 2 * W, C + 2 * W, 1, Y)
    de_s = f32(3, C + 2 * W, 1, Y)
    own_s = f32(L, C, T, Y)
    sent = call(
        functools.partial(own_body, dims, n_tile, n_lev),
        [f32(L, E, T, Y)] * n_tile + [f32(H + E + 1, lev_rows, Y)] * n_lev + [qe_s, ext_s, fe_s, de_s],
        [],
        [q, l, f, d],
    )
    qe, le, fe, de = sent[n_tile + n_lev :]
    from_lev = swap(sent[n_tile : n_tile + n_lev], "lev", lev_pairs)
    late_tile = swap(sent[:n_tile], "tile", tile_pairs)
    me, ky = call(functools.partial(inner_y_body, dims), [ext_s, f32(L, C, 3, T, Y)], [], [qe, fe, de])
    n = n_lev
    qe, le, fe, me, kv = call(
        functools.partial(inner_v_body, dims, n_lev),
        [qe_s, ext_s, fe_s, ext_s, f32(L + 2, C, 3, T, Y)],
        [],
        [*from_lev, qe, le, fe, me, de],
        aliases={n + i: i for i in range(4)},
    )
    to_lev = call(
        functools.partial(corner_body, dims, n_tile), [f32(n_tile, E, tile_rows, Y)] * n_lev, [], [*from_tile, me]
    )
    corners = swap(to_lev, "lev", lev_pairs)
    n = n_tile
    qe, fe, de, me, zc = call(
        functools.partial(beside_body, dims, n_tile),
        [qe_s, fe_s, de_s, ext_s, own_s],
        [],
        [*from_tile, qe, fe, de, me],
        aliases={n + i: i for i in range(4)},
    )
    n = n_lev + n_tile
    qe, le, fe, me, mc, late, *mc_edges = call(
        functools.partial(late_body, dims, n_tile, n_lev),
        [qe_s, ext_s, fe_s, ext_s, own_s, f32(3, L, C, Y)] + [f32(L, E, T, Y)] * n_tile,
        [],
        [*corners, *late_tile, de, qe, le, fe, me],
        aliases={n + 1 + i: i for i in range(4)},
    )
    mc_tile = swap(mc_edges, "tile", tile_pairs)
    mc, late, *mc_edges = call(
        functools.partial(late_inner_body, dims),
        [own_s, f32(3, L, C, Y)] + [f32(E, C, T, Y)] * n_lev,
        [],
        [le, fe, de, me, mc, late],
        aliases={4: 0, 5: 1},
    )
    mc_lev = swap(mc_edges, "lev", lev_pairs)
    le, acc = call(functools.partial(start_inner_body, dims), [ext_s, own_s], [], [qe, fe, de, mc, ky])
    le, speeds = call(
        functools.partial(start_levels_body, dims, n_lev),
        [ext_s, f32(3, L, C, Y)],
        [],
        [fe, de, kv, ky, zc, late, *mc_lev, le],
        aliases={6 + n_lev: 0},
    )
    pair = lax.axis_size("trc") == 2 and L % 2 == 0
    le, speeds, *given = call(
        functools.partial(speeds_body, dims, n_tile),
        [ext_s] + ([f32(3, L // 2, C, Y)] * 2 if pair else [f32(3, L, C, Y)]),
        [pltpu.VMEM((L, Y), jnp.float32)],
        [fe, de, speeds, zc, *mc_tile, le],
        aliases={4 + n_tile: 0},
    )
    if pair:
        other = swap(given, "trc", [[(0, 1), (1, 0)]])[0]
    start, _ = call(
        functools.partial(start_edge_body, dims),
        [f32(T, L, C, Y), own_s],
        [pltpu.VMEM((T, L, C, Y), jnp.float32), pltpu.SemaphoreType.DMA((L,))],
        [qe, fe, de, le, ky, kv, acc],
        aliases={6: 1},
        hbm_out=1,
    )
    speeds = speeds + other if pair else lax.psum_scatter(speeds, "trc", scatter_dimension=1, tiled=True)
    return start, speeds


def solution(mesh):
    return jax.shard_map(
        program,
        mesh=mesh,
        in_specs=(
            P("trc", "lev", ("ens", "tile"), None),
            P("trc", "lev", ("ens", "tile"), None),
            P("lev", ("ens", "tile"), None),
            P("lev", ("ens", "tile"), None),
            P("lev", ("ens", "tile"), None),
            P("lev", ("ens", "tile"), None),
            P("lev", ("ens", "tile"), None),
            P(("ens", "tile"), None),
        ),
        out_specs=(
            P("trc", "lev", ("ens", "tile"), None),
            P(None, ("lev", "trc"), ("ens", "tile"), None),
        ),
        check_vma=False,
    )
```
